256 devices in a mesh: et: 16 (over y, x), ex: 8 (over z), dp: 2 (over core).
Axes of the slice: x: 4, y: 4, z: 8, core: 2. Of those that a mesh axis runs over, the one named last changes fastest.
Arguments:
- tokens: bfloat16 [8192, 1664], P(('et', 'ex', 'dp')), may hold values from -6 to 6
- gate_probs: float32 [8192, 2], P(('et', 'ex', 'dp')), may hold values from 0.2 to 1
- expert_ids: int32 [8192, 2], P(('et', 'ex', 'dp')), may hold values from 0 to 15, as said below
- copies: int32 [16], replicated, may hold values from 1 to 2, as said below
- weight_in: bfloat16 [16, 1664, 8192], P('ex', None, ('et', 'dp')), may hold values from -0.15625 to 0.15625
- weight_out: bfloat16 [16, 8192, 1664], P('ex', ('et', 'dp')), may hold values from -0.0625 to 0.0625
- cotangent: bfloat16 [8192, 1664], P(('et', 'ex', 'dp')), may hold values from -6 to 6
Outputs:
- layer_out: bfloat16 [8192, 1664], P(('et', 'ex', 'dp'))
- grad_tokens: bfloat16 [8192, 1664], P(('et', 'ex', 'dp'))
- grad_gates: float32 [8192, 2], P(('et', 'ex', 'dp'))
- grad_weight_in: float32 [16, 1664, 8192], P('ex', None, ('et', 'dp'))
- grad_weight_out: float32 [16, 8192, 1664], P('ex', ('et', 'dp'))
The draws below stay inside these ranges and needn't reach their ends.
Inputs may be any that keep to these rules, and one draw needn't show every extreme that they name: `expert_ids`: the two experts of a token differ. Of each aligned run of 2 experts exactly one has 2 copies.
All inputs are finite; a program needn't handle non-finite values.
Results may differ from the reference program's by a relative error of at most 0.02.
Values may be sent and summed in bfloat16 or wider, within the bound.
A program may use at most 128 MiB of HBM per device.

```python
import jax
import jax.numpy as jnp
from jax import lax

D = 1664
FF = 8192
EXPERTS = 16
TOP = 2
TOK_DEV = 32
CAP = 2
EXP_GRP = 2
FF_DEV = 256
TOKENS = 8192
N_DP = 2


def pick_hot(key):
    return jax.random.randint(jax.random.fold_in(key, 9101), (), 0, EXPERTS)


def draw_copies(key, part):
    hot_id = pick_hot(key)
    group_total = EXPERTS // EXP_GRP
    chosen = jax.random.randint(jax.random.fold_in(key, 9102), (group_total,), 0, EXP_GRP)
    chosen = jnp.where(jnp.arange(group_total) == hot_id // EXP_GRP, hot_id % EXP_GRP, chosen)
    expert_range = jnp.arange(EXPERTS)
    doubled = expert_range % EXP_GRP == chosen[expert_range // EXP_GRP]
    return (1 + doubled.astype(jnp.int32)).astype(jnp.int32)


def block_pairs(key, hot_id, block_index):
    block_key = jax.random.fold_in(jax.random.fold_in(key, 9103), block_index)
    subkeys = jax.random.split(block_key, 5)
    expert_range = jnp.arange(EXPERTS)
    second = (hot_id + 1 + jax.random.randint(subkeys[0], (), 0, EXPERTS - 1)) % EXPERTS
    second_count = jax.random.randint(subkeys[1], (), 1, 2 * CAP + 1)
    random_ranks = jax.random.permutation(subkeys[2], EXPERTS)
    pushed = ((expert_range == hot_id) | (expert_range == second)).astype(jnp.int32)
    others = jnp.argsort(random_ranks + EXPERTS * pushed)
    places = jnp.arange(2 * TOK_DEV)
    cycled = others[(places - 2 * CAP - second_count) % (EXPERTS - 2)]
    labels = jnp.where(places < 2 * CAP, hot_id, jnp.where(places < 2 * CAP + second_count, second, cycled))
    labels = jnp.sort(labels)
    id_pairs = jnp.stack([labels[:TOK_DEV], labels[TOK_DEV:]], axis=1)
    id_pairs = id_pairs[jax.random.permutation(subkeys[3], TOK_DEV)]
    flip_bits = jax.random.randint(subkeys[4], (TOK_DEV, 1), 0, 2)
    return jnp.where(flip_bits == 1, id_pairs[:, ::-1], id_pairs)


def draw_expert_ids(key, part):
    hot_id = pick_hot(key)

    def one_block(block_index):
        return block_pairs(key, hot_id, block_index)
    id_pairs = jax.vmap(one_block)(jnp.arange(TOKENS // TOK_DEV))
    return id_pairs.reshape(TOKENS, 2).astype(jnp.int32)


def level_of(own_key, dims, cuts, low, high):
    def one(axis_at, shards_of):
        heights = jax.random.uniform(jax.random.fold_in(jax.random.fold_in(own_key, 6), axis_at), (shards_of,), jnp.float32, low / len(cuts), high / len(cuts))
        return jnp.repeat(jnp.exp(heights), dims[axis_at] // shards_of).reshape((-1,) + (1,) * (len(dims) - axis_at - 1))

    level = one(*cuts[0])
    for cut in cuts[1:]:
        level = level * one(*cut)
    return level


def gaussian(stream_key, dims, scale, limit, pieces=(), kind=jnp.bfloat16):
    entries = jax.random.normal(stream_key, dims, jnp.float32) * scale
    if len(pieces) > 0:
        entries = level_of(stream_key, dims, pieces, -0.22, 0.18) * entries
    return jnp.clip(entries, min=-limit, max=limit).astype(kind)


def setup_inputs(seed: int = 0) -> dict:
    splits = jax.random.split(jax.random.key(seed), 8)
    tokens = gaussian(splits[0], (TOKENS, D), 1.0, 6.0, ((0, 256),))
    gate_probs = jnp.clip(0.2 + 0.8 * jax.random.uniform(splits[1], (TOKENS, TOP), jnp.float32) ** level_of(splits[1], (TOKENS, TOP), ((0, 256),), -0.2, 0.2), 0.2, 1.0)
    expert_ids = draw_expert_ids(jax.random.fold_in(splits[7], 71), 0)
    copies = draw_copies(jax.random.fold_in(splits[7], 71), 0)
    weight_in = gaussian(splits[4], (EXPERTS, D, FF), D ** -0.5, 0.15625, ((0, 8), (2, 32)))
    weight_out = gaussian(splits[5], (EXPERTS, FF, D), FF ** -0.5, 0.0625, ((0, 8), (1, 32)))
    cotangent = gaussian(splits[6], (TOKENS, D), 1.0, 6.0, ((0, 256),))
    return dict(tokens=tokens, gate_probs=gate_probs, expert_ids=expert_ids, copies=copies, weight_in=weight_in, weight_out=weight_out, cotangent=cotangent)


gelu_scale = 0.7978845608028654


def gelu_tanh(values):
    inner_arg = gelu_scale * (values + 0.044715 * values * values * values)
    return 0.5 * values * (1.0 + jnp.tanh(inner_arg))


def gelu_slope(values):
    return jax.jvp(gelu_tanh, (values,), (jnp.ones_like(values),))[1]


def rounded(values):
    narrow = lax.optimization_barrier(values.astype(jnp.bfloat16))
    return narrow.astype(jnp.float32)


def block_table(block_ids, copies):
    flat_ids = block_ids.reshape(-1)
    labels = jnp.arange(EXPERTS, dtype=jnp.int32)
    onehot = (flat_ids[:, None] == labels[None, :]).astype(jnp.int32)
    earlier = jnp.cumsum(onehot, axis=0) - onehot
    ranking = jnp.sum(earlier * onehot, axis=1)
    allowed = CAP * jnp.sum(onehot * copies[None, :], axis=1)
    target = jnp.where(ranking < allowed, flat_ids * (2 * CAP) + ranking, -1)
    columns = jnp.arange(EXPERTS * 2 * CAP, dtype=jnp.int32)
    return (target[:, None] == columns[None, :]).astype(jnp.float32)


def one_expert(operands):
    inputs, upstream, weight_in, weight_out = operands
    portions = FF // FF_DEV
    highest = lax.Precision.HIGHEST
    flat_in = inputs.reshape(-1, D)
    flat_up = upstream.reshape(-1, D)
    pre_act = jnp.dot(flat_in, weight_in, preferred_element_type=jnp.float32)
    hidden = gelu_tanh(pre_act).astype(jnp.bfloat16)
    partials = jnp.einsum("rbf,bfd->rbd", hidden.reshape(-1, portions, FF_DEV).astype(jnp.float32),
                          weight_out.reshape(portions, FF_DEV, D).astype(jnp.float32), precision=highest)
    expert_out = jnp.sum(rounded(partials), axis=1).astype(jnp.bfloat16)
    back_hidden = jnp.dot(flat_up, weight_out.T, preferred_element_type=jnp.float32)
    slope_rows = (back_hidden * gelu_slope(pre_act)).astype(jnp.bfloat16)
    grad_parts = jnp.einsum("rbf,dbf->rbd", slope_rows.reshape(-1, portions, FF_DEV).astype(jnp.float32),
                            weight_in.reshape(D, portions, FF_DEV).astype(jnp.float32), precision=highest)
    input_grad = jnp.sum(rounded(grad_parts), axis=1).astype(jnp.bfloat16)
    replica_in = inputs.reshape(-1, N_DP, 2 * CAP, D).astype(jnp.float32)
    replica_up = upstream.reshape(-1, N_DP, 2 * CAP, D).astype(jnp.float32)
    replica_hidden = hidden.reshape(-1, N_DP, 2 * CAP, FF).astype(jnp.float32)
    replica_slope = slope_rows.reshape(-1, N_DP, 2 * CAP, FF).astype(jnp.float32)
    grad_in = jnp.sum(rounded(jnp.einsum("qrcd,qrcf->rdf", replica_in, replica_slope, precision=highest)), axis=0)
    grad_out = jnp.sum(rounded(jnp.einsum("qrcf,qrcd->rfd", replica_hidden, replica_up, precision=highest)), axis=0)
    return expert_out.reshape(inputs.shape), input_grad.reshape(inputs.shape), grad_in, grad_out


def reference(tokens, gate_probs, expert_ids, copies, weight_in, weight_out, cotangent):
    highest = lax.Precision.HIGHEST
    blocks = TOKENS // TOK_DEV

    def table_of(block_ids):
        return block_table(block_ids, copies)

    tables = jax.vmap(table_of)(expert_ids.reshape(blocks, TOK_DEV, TOP))
    token_rows = jnp.repeat(tokens, TOP, axis=0).astype(jnp.float32).reshape(blocks, TOK_DEV * TOP, D)
    upstream = (gate_probs.reshape(-1, 1) * jnp.repeat(cotangent, TOP, axis=0).astype(jnp.float32)).astype(jnp.bfloat16)
    up_rows = upstream.astype(jnp.float32).reshape(blocks, TOK_DEV * TOP, D)
    slot_in = jnp.einsum("bas,bad->bsd", tables, token_rows, precision=highest).astype(jnp.bfloat16)
    slot_up = jnp.einsum("bas,bad->bsd", tables, up_rows, precision=highest).astype(jnp.bfloat16)
    expert_in = slot_in.reshape(blocks, EXPERTS, 2 * CAP, D).transpose(1, 0, 2, 3)
    expert_up = slot_up.reshape(blocks, EXPERTS, 2 * CAP, D).transpose(1, 0, 2, 3)
    expert_out, input_grad, grad_weight_in, grad_weight_out = lax.map(
        one_expert, (expert_in, expert_up, weight_in, weight_out))
    out_slots = expert_out.transpose(1, 0, 2, 3).reshape(blocks, EXPERTS * 2 * CAP, D).astype(jnp.float32)
    assigned = jnp.einsum("bas,bsd->bad", tables, out_slots, precision=highest).reshape(TOKENS, TOP, D)
    layer_out = jnp.sum(gate_probs[:, :, None] * assigned, axis=1).astype(jnp.bfloat16)
    grad_gates = jnp.sum(cotangent.astype(jnp.float32)[:, None, :] * assigned, axis=2)
    grad_slots = input_grad.transpose(1, 0, 2, 3).reshape(blocks, EXPERTS * 2 * CAP, D).astype(jnp.float32)
    grad_assigned = jnp.einsum("bas,bsd->bad", tables, grad_slots, precision=highest).reshape(TOKENS, TOP, D)
    grad_tokens = jnp.sum(grad_assigned, axis=1).astype(jnp.bfloat16)
    return layer_out, grad_tokens, grad_gates, grad_weight_in, grad_weight_out
```

```python
import functools

import jax
import jax.numpy as jnp
import numpy as np
from jax import lax
from jax.experimental import pallas as pl
from jax.experimental.pallas import tpu as pltpu
from jax.sharding import PartitionSpec as P

MESH = pl.DeviceIdType.MESH
SIDE = 4
UNITS = SIDE * SIDE
FRAME = 16
SLOTS = 6
DELTAS = (0, -1, 1, 2)
F32 = jnp.float32
BF16 = jnp.bfloat16
gelu_scale = 0.7978845608028654


def pack_matrix(groups):
    single, doubled = 2 * groups, 4 * groups
    out = np.zeros((2 * (single + doubled), groups * FRAME), np.float32)
    for kind in range(2):
        for r in range(single):
            out[kind * (single + doubled) + r, (r // 2) * FRAME + kind * SLOTS + r % 2] = 1
        for r in range(doubled):
            out[kind * (single + doubled) + single + r, (r // 4) * FRAME + kind * SLOTS + 2 + r % 4] = 1
    return out


def column_tiles(width, step):
    return [(c, min(step, width - c)) for c in range(0, width, step)]


def layer_kernel(
    groups, copies_ref, select_ref, pack_ref, tokens_ref, cot_ref, gates_ref, wi_hbm, wo_hbm,
    layer_ref, gtok_ref, ggate_ref, gi_own_hbm, gi_got_hbm, go_own_hbm, go_got_hbm,
    wi, wo, frames, zin, xr, part, rbuf, own, frames_back, zback, hid, slope_v, dgelu, gi_v, go_v,
    w_send, w_recv, w_load, z_send, z_recv, ag_send, ag_recv, rs_send, rs_recv, zb_send, zb_recv, g_send, g_recv, g_store,
):
    width = tokens_ref.shape[1]
    hidden = wi.shape[3]
    et = lax.axis_index("et")
    ex = lax.axis_index("ex")
    dp = lax.axis_index("dp")
    y, x = lax.div(et, SIDE), lax.rem(et, SIDE)
    other = 1 - dp
    kind_rows = 6 * groups
    single = 2 * groups
    half_cut = (width // 128 + 1) // 2 * 128
    doubled = jnp.where(copies_ref[2 * ex + 1] == 2, 1, 0)

    def step_of(v, d):
        return lax.rem(v + (d + SIDE), SIDE)

    def unit_of(h, b, a):
        return b * SIDE + a if h == 0 else a * SIDE + b

    barrier = pltpu.get_barrier_semaphore()
    for dev in (
        unit_of(0, y, step_of(x, 1)), unit_of(0, y, step_of(x, -1)),
        unit_of(0, step_of(y, 1), x), unit_of(0, step_of(y, -1), x),
    ):
        pl.semaphore_signal(barrier, inc=1, device_id={"et": dev}, device_id_type=MESH)
    for o in range(1, groups):
        pl.semaphore_signal(barrier, inc=1, device_id={"ex": lax.rem(ex + o, groups)}, device_id_type=MESH)
    pl.semaphore_signal(barrier, inc=1, device_id={"dp": other}, device_id_type=MESH)

    loads = [
        pltpu.make_async_copy(wi_hbm, wi.at[0], w_load.at[0]),
        pltpu.make_async_copy(wo_hbm, wo.at[0], w_load.at[1]),
    ]
    for c in loads:
        c.start()

    cot = cot_ref[...].astype(F32)
    up0 = (cot * gates_ref[:, 0:1]).astype(BF16)
    up1 = (cot * gates_ref[:, 1:2]).astype(BF16)
    stacked = jnp.concatenate([tokens_ref[...], up0, up1], axis=0)
    made = jnp.dot(select_ref[...], stacked, preferred_element_type=F32).astype(BF16)
    frames[...] = made.reshape(groups, FRAME, width)

    pl.semaphore_wait(barrier, 4 + groups - 1 + 1)

    def z_copy(o, src, dst, send, recv):
        peer = lax.rem(ex + o, groups)
        return pltpu.make_async_remote_copy(
            src_ref=src.at[peer], dst_ref=dst.at[ex], send_sem=send, recv_sem=recv.at[ex],
            device_id={"ex": peer}, device_id_type=MESH,
        )

    def z_exchange(src, dst, send, recv):
        for o in range(1, groups):
            z_copy(o, src, dst, send, recv).start()
        dst[ex] = src[ex]

    def z_arrived(src, dst, send, recv):
        for o in range(1, groups):
            peer = lax.rem(ex + o, groups)
            pltpu.make_async_copy(src.at[peer], dst.at[peer], recv.at[peer]).wait()
        pltpu.make_async_copy(src.at[pl.ds(0, groups - 1)], dst.at[pl.ds(0, groups - 1)], send).wait()

    z_exchange(frames, zin, z_send, z_recv)
    swaps = [
        pltpu.make_async_remote_copy(
            src_ref=hbm, dst_ref=v.at[1], send_sem=w_send.at[i], recv_sem=w_recv.at[i],
            device_id={"dp": other}, device_id_type=MESH,
        )
        for i, (hbm, v) in enumerate(((wi_hbm, wi), (wo_hbm, wo)))
    ]
    for c in swaps:
        c.start()
    z_arrived(frames, zin, z_send, z_recv)

    def halves(h):
        return (x, y, 0, half_cut) if h == 0 else (y, x, half_cut, width - half_cut)

    def part_rows(k, p):
        cut = single if k == 0 else 2 * single
        return (0, cut) if p == 0 else (cut, kind_rows - cut)

    class Gather:
        def __init__(self, k, h):
            self.k, self.h = k, h
            self.a, self.b, self.c0, self.cn = halves(h)

        def ref(self, u, r0=0, rn=None):
            rn = kind_rows if rn is None else rn
            return xr.at[u, pl.ds(self.k * kind_rows + r0, rn), pl.ds(self.c0, self.cn)]

        def unit(self, db, da):
            return unit_of(self.h, step_of(self.b, db), step_of(self.a, da))

        def send(self, u, db, da, ident, rows=(0, None)):
            ref = self.ref(u, *rows)
            pltpu.make_async_remote_copy(
                src_ref=ref, dst_ref=ref, send_sem=ag_send, recv_sem=ag_recv.at[self.k, self.h, ident],
                device_id={"et": self.unit(db, da)}, device_id_type=MESH,
            ).start()

        def wait(self, u, ident, rows=(0, None)):
            ref = self.ref(u, *rows)
            pltpu.make_async_copy(ref, ref, ag_recv.at[self.k, self.h, ident]).wait()

        def start(self):
            u = self.unit(0, 0)
            self.send(u, 0, 1, 0)
            self.send(u, 0, -1, 1)
            self.send(u, 1, 0, 4)
            self.send(u, -1, 0, 8)

        def near(self):
            u = self.unit(0, -1)
            self.wait(u, 0)
            self.send(u, 0, 1, 2, part_rows(self.k, 0))
            self.send(u, 1, 0, 5)
            self.send(u, -1, 0, 9)
            u = self.unit(0, 1)
            self.wait(u, 1)
            self.send(u, 0, -1, 3, part_rows(self.k, 1))
            self.send(u, 1, 0, 6)
            self.send(u, -1, 0, 10)

        def far(self):
            u = self.unit(0, 2)
            self.wait(u, 2, part_rows(self.k, 0))
            self.wait(u, 3, part_rows(self.k, 1))
            self.send(u, 1, 0, 7)
            self.send(u, -1, 0, 11)

        def cross(self):
            for j, d in enumerate(DELTAS):
                u = self.unit(-1, d)
                self.wait(u, 4 + j)
                if j < 2:
                    self.send(u, 1, 0, 12 + j)
                u = self.unit(1, d)
                self.wait(u, 8 + j)
                if j >= 2:
                    self.send(u, -1, 0, 12 + j)

        def last(self):
            for j, d in enumerate(DELTAS):
                self.wait(self.unit(2, d), 12 + j)

    packed = jnp.dot(pack_ref[...], zin[...].reshape(groups * FRAME, width), preferred_element_type=F32)
    xr[et] = packed.astype(BF16)

    g_in = [Gather(0, h) for h in range(2)]
    g_up = [Gather(1, h) for h in range(2)]
    for g in g_in:
        g.start()
    for g in g_in:
        g.near()
    for g in g_up:
        g.start()
    for g in g_in:
        g.far()
    for g in g_up:
        g.near()
    for g in g_in:
        g.cross()
    for g in g_up:
        g.far()
    for g in g_in:
        g.last()
    for g in g_up:
        g.cross()
    for g in g_up:
        g.last()
    for c in loads:
        c.wait()
    for c in swaps:
        c.wait()

    half_units = UNITS // 2
    chunks = [
        (1 - doubled, 0, UNITS, 0, single, 0),
        (doubled, 0, half_units, single, 2 * single, UNITS * single),
        (doubled, half_units, half_units, single, 2 * single, 2 * UNITS * single),
    ]
    rows = UNITS * single
    tiles = column_tiles(width, 256)
    full_tiles = width // 256

    def over_tiles(body):
        def step(i, carry):
            body(pl.multiple_of(i * 256, 256), 256)
            return carry

        lax.fori_loop(0, full_tiles, step, 0)
        if width % 256:
            body(full_tiles * 256, width % 256)

    def block(ref, chunk, kind, c0=None, cn=None):
        _, u0, un, r0, rn, _ = chunk
        cols = slice(None) if c0 is None else pl.ds(c0, cn)
        return ref[pl.ds(u0, un), pl.ds(kind * kind_rows + r0, rn), cols].reshape(un * rn, width if c0 is None else cn)

    def put(ref, chunk, kind, c0, cn, value):
        _, u0, un, r0, rn, _ = chunk
        ref[pl.ds(u0, un), pl.ds(kind * kind_rows + r0, rn), pl.ds(c0, cn)] = value.reshape(un, rn, cn)

    for chunk in chunks:
        e, at = chunk[0], chunk[5]
        for q in range(2):
            v = jnp.dot(block(xr, chunk, 0), wi[q, e], preferred_element_type=F32)
            square = v * v
            t = jnp.tanh(gelu_scale * (v + 0.044715 * square * v))
            hid[pl.ds(at, rows), q * hidden:(q + 1) * hidden] = (0.5 * v * (1.0 + t)).astype(BF16)
            dgelu[pl.ds(at, rows), q * hidden:(q + 1) * hidden] = 0.5 * (1.0 + t) + 0.5 * v * (1.0 - t * t) * (
                gelu_scale * (1.0 + 3 * 0.044715 * square)
            )

    for chunk in chunks:
        e, at = chunk[0], chunk[5]

        def out_tile(c0, cn, chunk=chunk, e=e, at=at):
            total = jnp.dot(hid[pl.ds(at, rows), 0:hidden], wo[0, e, :, pl.ds(c0, cn)], preferred_element_type=F32)
            total += jnp.dot(hid[pl.ds(at, rows), hidden:2 * hidden], wo[1, e, :, pl.ds(c0, cn)], preferred_element_type=F32)
            put(part, chunk, 1, c0, cn, total.astype(BF16))

        over_tiles(out_tile)

    class Scatter:
        def __init__(self, k, h):
            self.k, self.h = k, h
            self.a, self.b, self.c0, self.cn = halves(h)

        def ref(self, u, r0=0, rn=None):
            rn = kind_rows if rn is None else rn
            return part.at[u, pl.ds(self.k * kind_rows + r0, rn), pl.ds(self.c0, self.cn)]

        def buf(self, slot, r0=0, rn=None):
            rn = kind_rows if rn is None else rn
            return rbuf.at[self.k, slot, pl.ds(r0, rn), pl.ds(self.c0, self.cn)]

        def unit(self, db, da):
            return unit_of(self.h, step_of(self.b, db), step_of(self.a, da))

        def send(self, u, db, da, slot, ident, rows=(0, None)):
            pltpu.make_async_remote_copy(
                src_ref=self.ref(u, *rows), dst_ref=self.buf(slot, *rows), send_sem=rs_send,
                recv_sem=rs_recv.at[self.k, self.h, ident],
                device_id={"et": self.unit(db, da)}, device_id_type=MESH,
            ).start()

        def wait(self, slot, ident, rows=(0, None)):
            ref = self.buf(slot, *rows)
            pltpu.make_async_copy(ref, ref, rs_recv.at[self.k, self.h, ident]).wait()

        def add(self, u, slots, rows=(0, None)):
            ref = self.ref(u, *rows)
            total = ref[...].astype(F32)
            for s in slots:
                total += self.buf(s, *rows)[...].astype(F32)
            ref[...] = total.astype(BF16)

        def start(self):
            for j, d in enumerate(DELTAS):
                self.send(self.unit(2, d), 1 if j < 2 else -1, 0, j, j)
            for j, d in enumerate(DELTAS):
                if j < 2:
                    self.send(self.unit(-1, d), -1, 0, 8 + j, 8 + j)
                else:
                    self.send(self.unit(1, d), 1, 0, 4 + j, 4 + j)

        def near(self):
            for j, d in enumerate(DELTAS):
                side = 1 if j < 2 else -1
                u = self.unit(side, d)
                self.wait(j, j)
                self.add(u, (j,))
                ident = (4 if j < 2 else 8) + j
                self.send(u, side, 0, ident, ident)

        def cross(self):
            for j in (3, 1, 2, 0):
                u = self.unit(0, DELTAS[j])
                self.wait(4 + j, 4 + j)
                self.wait(8 + j, 8 + j)
                self.add(u, (4 + j, 8 + j))
                if j == 3:
                    self.send(u, 0, 1, 12, 12, part_rows(self.k, 0))
                    self.send(u, 0, -1, 12, 13, part_rows(self.k, 1))

        def far(self):
            for p, side in ((0, 1), (1, -1)):
                u = self.unit(0, side)
                piece = part_rows(self.k, p)
                self.wait(12, 12 + p, piece)
                self.add(u, (12,), piece)
                self.send(u, 0, side, 13 + p, 14 + p)

        def last(self):
            self.wait(13, 14)
            self.wait(14, 15)
            total = self.ref(self.unit(0, 0))[...].astype(F32)
            for s in (13, 14):
                total += self.buf(s)[...].astype(F32)
            own[pl.ds(self.k * kind_rows, kind_rows), pl.ds(self.c0, self.cn)] = total.astype(BF16)

    s_in = [Scatter(0, h) for h in range(2)]
    s_out = [Scatter(1, h) for h in range(2)]
    for s in s_out:
        s.start()

    for chunk in chunks:
        e, at = chunk[0], chunk[5]
        for q in range(2):
            back = lax.dot_general(block(xr, chunk, 1), wo[q, e], (((1,), (1,)), ((), ())), preferred_element_type=F32)
            slope_v[pl.ds(at, rows), q * hidden:(q + 1) * hidden] = (
                back * dgelu[pl.ds(at, rows), q * hidden:(q + 1) * hidden]
            ).astype(BF16)

    for s in s_out:
        s.near()

    for chunk in chunks:
        e, at = chunk[0], chunk[5]

        def grad_tile(c0, cn, chunk=chunk, e=e, at=at):
            total = None
            for q in range(2):
                term = lax.dot_general(
                    slope_v[pl.ds(at, rows), q * hidden:(q + 1) * hidden], wi[q, e, pl.ds(c0, cn), :],
                    (((1,), (1,)), ((), ())), preferred_element_type=F32,
                )
                total = term if total is None else total + term
            put(part, chunk, 0, c0, cn, total.astype(BF16))

        over_tiles(grad_tile)

    for s in s_in:
        s.start()
    for s in s_out:
        s.cross()

    first_doubled = doubled == 0

    def tn(lhs, rhs):
        return lax.dot_general(lhs, rhs, (((0,), (0,)), ((), ())), preferred_element_type=F32)

    def whole(kind, role, c0, cn):
        r0, rn = (0, single) if role == 0 else (single, 2 * single)
        return xr[:, pl.ds(kind * kind_rows + r0, rn), pl.ds(c0, cn)].reshape(UNITS * rn, cn)

    def role_rows(ref, role):
        return ref[0:rows, :] if role == 0 else ref[rows:3 * rows, :]

    def gi_tile(c0, cn):
        by_role = [tn(whole(0, role, c0, cn), role_rows(slope_v, role)) for role in range(2)]
        for e in range(2):
            value = jnp.where(first_doubled, by_role[1 - e], by_role[e]).astype(BF16)
            for q in range(2):
                gi_v[q, e, pl.ds(c0, cn), :] = value[:, q * hidden:(q + 1) * hidden]

    def go_tile(c0, cn):
        by_role = [tn(role_rows(hid, role), whole(1, role, c0, cn)) for role in range(2)]
        for e in range(2):
            value = jnp.where(first_doubled, by_role[1 - e], by_role[e]).astype(BF16)
            for q in range(2):
                go_v[q, e, :, pl.ds(c0, cn)] = value[q * hidden:(q + 1) * hidden, :]

    def give(i, v, own_hbm, got_hbm):
        store = pltpu.make_async_copy(v.at[0], own_hbm, g_store.at[i])
        swap = pltpu.make_async_remote_copy(
            src_ref=v.at[1], dst_ref=got_hbm, send_sem=g_send.at[i], recv_sem=g_recv.at[i],
            device_id={"dp": other}, device_id_type=MESH,
        )
        store.start()
        swap.start()
        return store, swap

    over_tiles(go_tile)
    given = [give(0, go_v, go_own_hbm, go_got_hbm)]
    for s in s_out:
        s.far()
    for s in s_in:
        s.near()
    over_tiles(gi_tile)
    given.append(give(1, gi_v, gi_own_hbm, gi_got_hbm))
    for s in s_out:
        s.last()
    for s in s_in:
        s.cross()
    for s in s_in:
        s.far()
    for s in s_in:
        s.last()

    frames_back[...] = tn(pack_ref[...], own[...]).astype(BF16).reshape(groups, FRAME, width)
    z_exchange(frames_back, zback, zb_send, zb_recv)
    z_arrived(frames_back, zback, zb_send, zb_recv)
    result = tn(select_ref[...], zback[...].reshape(groups * FRAME, width))
    count = tokens_ref.shape[0]
    gtok_ref[...] = result[0:count].astype(BF16)
    first, second = result[count:2 * count], result[2 * count:3 * count]
    layer_ref[...] = (gates_ref[:, 0:1] * first + gates_ref[:, 1:2] * second).astype(BF16)
    ggate_ref[:, 0:1] = jnp.sum(cot * first, axis=1, keepdims=True)
    ggate_ref[:, 1:2] = jnp.sum(cot * second, axis=1, keepdims=True)

    sent = xr.at[pl.ds(0, UNITS - 1)]
    pltpu.make_async_copy(sent, sent, ag_send).wait()
    sent = part.at[pl.ds(0, UNITS - 1)]
    pltpu.make_async_copy(sent, sent, rs_send).wait()
    for store, swap in given:
        store.wait()
        swap.wait()


def selection(expert_ids, copies, groups):
    count = expert_ids.shape[0]
    pair = jnp.arange(2 * groups, dtype=jnp.int32)
    spots = jnp.arange(groups * FRAME, dtype=jnp.int32)[:, None]
    order = jnp.arange(count, dtype=jnp.int32)
    earlier = order[None, :] < order[:, None]
    places = []
    for k in range(2):
        ids = expert_ids[:, k]
        same = (ids[:, None] == expert_ids[None, :, 0]).astype(jnp.int32) + (
            ids[:, None] == expert_ids[None, :, 1]
        ).astype(jnp.int32)
        rank = jnp.sum(jnp.where(earlier, same, 0), axis=1)
        held = jnp.sum(jnp.where(ids[:, None] == pair[None, :], copies[None, :], 0), axis=1)
        spot = (ids // 2) * FRAME + jnp.where(held == 2, 2 + rank, rank)
        places.append(jnp.where(rank < 2 * held, spot, -FRAME))
    first, second = places
    token_rows = (spots == first[None, :]) | (spots == second[None, :])
    return jnp.concatenate(
        [token_rows, spots == first[None, :] + SLOTS, spots == second[None, :] + SLOTS], axis=1
    ).astype(BF16)


def shards(mesh_shape, tokens, gate_probs, expert_ids, copies, weight_in, weight_out, cotangent):
    groups = mesh_shape["ex"]
    count, width = tokens.shape
    hidden = weight_in.shape[2]
    unit_rows = 12 * groups
    kind_rows = 6 * groups
    all_rows = UNITS * kind_rows
    select = selection(expert_ids, copies, groups)
    pack = jnp.asarray(pack_matrix(groups), BF16)
    vmem, anywhere = pl.BlockSpec(memory_space=pltpu.VMEM), pl.BlockSpec(memory_space=pl.ANY)
    shape = jax.ShapeDtypeStruct
    dma = pltpu.SemaphoreType.DMA
    results = pl.pallas_call(
        functools.partial(layer_kernel, groups),
        out_shape=(
            shape((count, width), BF16), shape((count, width), BF16), shape((count, 2), F32),
            shape(weight_in.shape, BF16), shape(weight_in.shape, BF16),
            shape(weight_out.shape, BF16), shape(weight_out.shape, BF16),
        ),
        in_specs=[pl.BlockSpec(memory_space=pltpu.SMEM), vmem, vmem, vmem, vmem, vmem, anywhere, anywhere],
        out_specs=(vmem, vmem, vmem, anywhere, anywhere, anywhere, anywhere),
        scratch_shapes=[
            pltpu.VMEM((2,) + weight_in.shape, BF16),
            pltpu.VMEM((2,) + weight_out.shape, BF16),
            pltpu.VMEM((groups, FRAME, width), BF16),
            pltpu.VMEM((groups, FRAME, width), BF16),
            pltpu.VMEM((UNITS, unit_rows, width), BF16),
            pltpu.VMEM((UNITS, unit_rows, width), BF16),
            pltpu.VMEM((2, 15, kind_rows, width), BF16),
            pltpu.VMEM((unit_rows, width), BF16),
            pltpu.VMEM((groups, FRAME, width), BF16),
            pltpu.VMEM((groups, FRAME, width), BF16),
            pltpu.VMEM((all_rows, 2 * hidden), BF16),
            pltpu.VMEM((all_rows, 2 * hidden), BF16),
            pltpu.VMEM((all_rows, 2 * hidden), F32),
            pltpu.VMEM((2,) + weight_in.shape, BF16),
            pltpu.VMEM((2,) + weight_out.shape, BF16),
            dma((2,)), dma((2,)), dma((2,)),
            dma(()), dma((groups,)),
            dma(()), dma((2, 2, 16)),
            dma(()), dma((2, 2, 16)),
            dma(()), dma((groups,)),
            dma((2,)), dma((2,)), dma((2,)),
        ],
        compiler_params=pltpu.CompilerParams(
            collective_id=0, has_side_effects=True, vmem_limit_bytes=60 * 2**20
        ),
        name="moe_layer",
    )(copies, select, pack, tokens, cotangent, gate_probs, weight_in, weight_out)
    layer_out, grad_tokens, grad_gates, gi_own, gi_got, go_own, go_got = results
    return (
        layer_out,
        grad_tokens,
        grad_gates,
        gi_own.astype(F32) + gi_got.astype(F32),
        go_own.astype(F32) + go_got.astype(F32),
    )


def solution(mesh):
    rows = P(("et", "ex", "dp"), None)
    w_in = P("ex", None, ("et", "dp"))
    w_out = P("ex", ("et", "dp"), None)
    return jax.shard_map(
        functools.partial(shards, dict(mesh.shape)),
        mesh=mesh,
        in_specs=(rows, rows, rows, P(), w_in, w_out, rows),
        out_specs=(rows, rows, rows, w_in, w_out),
        check_vma=False,
    )
```

```python
import functools

import jax
import jax.numpy as jnp
import numpy as np
from jax import lax
from jax.experimental import pallas as pl
from jax.experimental.pallas import tpu as pltpu
from jax.sharding import PartitionSpec as P

MESH = pl.DeviceIdType.MESH
SIDE = 4
UNITS = SIDE * SIDE
FRAME = 8
DELTAS = (0, -1, 1, 2)
F32 = jnp.float32
BF16 = jnp.bfloat16
gelu_scale = 0.7978845608028654


def pack_matrix(groups):
    single = 2 * groups
    out = np.zeros((3 * single, groups * FRAME), np.float32)
    for r in range(single):
        out[r, (r // 2) * FRAME + r % 2] = 1
    for r in range(2 * single):
        out[single + r, (r // 4) * FRAME + 2 + r % 4] = 1
    return out


def column_tiles(width, step):
    return [(c, min(step, width - c)) for c in range(0, width, step)]


def layer_kernel(
    groups, ids_hbm, copies_hbm, pack_hbm, tokens_hbm, cot_hbm, gates_hbm, wi_hbm, wo_hbm,
    layer_ref, gtok_ref, ggate_ref, gi_own_hbm, gi_got_hbm, go_own_hbm, go_got_hbm,
    ids_ref, copies_ref, pack_ref, tokens_ref, cot_ref, gates_ref, wi, wo, frames, zin, xr, part, rbuf, own, frames_back, zback, hid, slope_v, dgelu, gi_v, go_v,
    in_load, w_send, w_recv, w_load, z_send, z_recv, ag_send, ag_recv, rs_send, rs_recv, zb_send, zb_recv, g_send, g_recv, g_store,
):
    width = tokens_ref.shape[1]
    hidden = wi.shape[3]
    et = lax.axis_index("et")
    ex = lax.axis_index("ex")
    dp = lax.axis_index("dp")
    y, x = lax.div(et, SIDE), lax.rem(et, SIDE)
    other = 1 - dp
    kind_rows = 6 * groups
    single = 2 * groups
    half_cut = (width // 128 + 1) // 2 * 128

    def step_of(v, d):
        return lax.rem(v + (d + SIDE), SIDE)

    def unit_of(h, b, a):
        return b * SIDE + a if h == 0 else a * SIDE + b

    arrays = [
        pltpu.make_async_copy(hbm, v, in_load.at[i])
        for i, (hbm, v) in enumerate((
            (ids_hbm, ids_ref), (copies_hbm, copies_ref), (gates_hbm, gates_ref),
            (cot_hbm, cot_ref), (tokens_hbm, tokens_ref), (pack_hbm, pack_ref),
        ))
    ]
    for c in arrays:
        c.start()

    barrier = pltpu.get_barrier_semaphore()
    for dev in (
        unit_of(0, y, step_of(x, 1)), unit_of(0, y, step_of(x, -1)),
        unit_of(0, step_of(y, 1), x), unit_of(0, step_of(y, -1), x),
    ):
        pl.semaphore_signal(barrier, inc=1, device_id={"et": dev}, device_id_type=MESH)
    for o in range(1, groups):
        pl.semaphore_signal(barrier, inc=1, device_id={"ex": lax.rem(ex + o, groups)}, device_id_type=MESH)
    pl.semaphore_signal(barrier, inc=1, device_id={"dp": other}, device_id_type=MESH)

    loads = [
        pltpu.make_async_copy(wi_hbm, wi.at[0], w_load.at[0]),
        pltpu.make_async_copy(wo_hbm, wo.at[0], w_load.at[1]),
    ]
    for c in loads:
        c.start()

    for c in arrays:
        c.wait()
    doubled = jnp.where(copies_ref[2 * ex + 1] == 2, 1, 0)
    count = tokens_ref.shape[0]
    square = (count, count)
    down, along = lax.broadcasted_iota(jnp.int32, square, 0), lax.broadcasted_iota(jnp.int32, square, 1)
    diagonal = down == along

    def upright(row):
        return jnp.sum(jnp.where(diagonal, jnp.broadcast_to(row, square), 0.0), axis=1, keepdims=True)

    def lying(column):
        return jnp.sum(jnp.where(diagonal, jnp.broadcast_to(column, square), 0.0), axis=0, keepdims=True)

    ids = [ids_ref[k:k + 1, :] for k in range(2)]
    columns = [upright(v.astype(F32)) for v in ids]
    spots = lax.broadcasted_iota(jnp.int32, (groups * FRAME, count), 0)
    chosen = []
    for k in range(2):
        mine = ids[k].astype(F32)
        same = sum(jnp.where((c == mine) & (down < along), 1.0, 0.0) for c in columns)
        rank = jnp.sum(same, axis=0, keepdims=True).astype(jnp.int32)
        held = jnp.zeros_like(ids[k])
        for e in range(2 * groups):
            held = jnp.where(ids[k] == e, copies_ref[e], held)
        spot = (ids[k] >> 1) * FRAME + jnp.where(held == 2, 2 + rank, rank)
        spot = jnp.where(rank < 2 * held, spot, -1)
        chosen.append(jnp.where(spots == spot, 1.0, 0.0).astype(BF16))
    either = chosen[0] + chosen[1]
    gates = [upright(gates_ref[k:k + 1, :]) for k in range(2)]
    cot = cot_ref[...].astype(F32)

    def fill(kind, value):
        frames[kind] = value.astype(BF16).reshape(groups, FRAME, width)

    fill(0, jnp.dot(either, tokens_ref[...], preferred_element_type=F32))
    fill(1, sum(jnp.dot(c, (cot * g).astype(BF16), preferred_element_type=F32) for c, g in zip(chosen, gates)))

    pl.semaphore_wait(barrier, 4 + groups - 1 + 1)

    def z_exchange(kind, src, dst, send, recv):
        for o in range(1, groups):
            peer = lax.rem(ex + o, groups)
            pltpu.make_async_remote_copy(
                src_ref=src.at[kind, peer], dst_ref=dst.at[kind, ex], send_sem=send.at[kind], recv_sem=recv.at[kind, ex],
                device_id={"ex": peer}, device_id_type=MESH,
            ).start()
        dst[kind, ex] = src[kind, ex]

    def z_arrived(kind, src, dst, send, recv):
        for o in range(1, groups):
            peer = lax.rem(ex + o, groups)
            pltpu.make_async_copy(src.at[kind, peer], dst.at[kind, peer], recv.at[kind, peer]).wait()
        sent = src.at[kind, pl.ds(0, groups - 1)]
        pltpu.make_async_copy(sent, sent, send.at[kind]).wait()

    z_exchange(0, frames, zin, z_send, z_recv)
    swaps = [
        pltpu.make_async_remote_copy(
            src_ref=hbm, dst_ref=v.at[1], send_sem=w_send.at[i], recv_sem=w_recv.at[i],
            device_id={"dp": other}, device_id_type=MESH,
        )
        for i, (hbm, v) in enumerate(((wi_hbm, wi), (wo_hbm, wo)))
    ]

    def halves(h):
        return (x, y, 0, half_cut) if h == 0 else (y, x, half_cut, width - half_cut)

    def part_rows(k, p):
        cut = single if k == 0 else 2 * single
        return (0, cut) if p == 0 else (cut, kind_rows - cut)

    class Gather:
        def __init__(self, k, h):
            self.k, self.h = k, h
            self.a, self.b, self.c0, self.cn = halves(h)

        def ref(self, u, r0=0, rn=None):
            rn = kind_rows if rn is None else rn
            return xr.at[u, pl.ds(self.k * kind_rows + r0, rn), pl.ds(self.c0, self.cn)]

        def unit(self, db, da):
            return unit_of(self.h, step_of(self.b, db), step_of(self.a, da))

        def send(self, u, db, da, ident, rows=(0, None)):
            ref = self.ref(u, *rows)
            pltpu.make_async_remote_copy(
                src_ref=ref, dst_ref=ref, send_sem=ag_send, recv_sem=ag_recv.at[self.k, self.h, ident],
                device_id={"et": self.unit(db, da)}, device_id_type=MESH,
            ).start()

        def wait(self, u, ident, rows=(0, None)):
            ref = self.ref(u, *rows)
            pltpu.make_async_copy(ref, ref, ag_recv.at[self.k, self.h, ident]).wait()

        def start(self):
            u = self.unit(0, 0)
            self.send(u, 0, 1, 0)
            self.send(u, 0, -1, 1)
            self.send(u, 1, 0, 4)
            self.send(u, -1, 0, 8)

        def near(self):
            u = self.unit(0, -1)
            self.wait(u, 0)
            self.send(u, 0, 1, 2, part_rows(self.k, 0))
            self.send(u, 1, 0, 5)
            self.send(u, -1, 0, 9)
            u = self.unit(0, 1)
            self.wait(u, 1)
            self.send(u, 0, -1, 3, part_rows(self.k, 1))
            self.send(u, 1, 0, 6)
            self.send(u, -1, 0, 10)

        def far(self):
            u = self.unit(0, 2)
            self.wait(u, 2, part_rows(self.k, 0))
            self.wait(u, 3, part_rows(self.k, 1))
            self.send(u, 1, 0, 7)
            self.send(u, -1, 0, 11)

        def cross(self, j):
            d = DELTAS[j]
            u = self.unit(-1, d)
            self.wait(u, 4 + j)
            if j < 2:
                self.send(u, 1, 0, 12 + j)
            u = self.unit(1, d)
            self.wait(u, 8 + j)
            if j >= 2:
                self.send(u, -1, 0, 12 + j)

        def last(self):
            for j, d in enumerate(DELTAS):
                self.wait(self.unit(2, d), 12 + j)

    def unpack(kind):
        rows_of_kind = jnp.dot(pack_ref[...], zin[kind].reshape(groups * FRAME, width), preferred_element_type=F32)
        xr[et, pl.ds(kind * kind_rows, kind_rows), :] = rows_of_kind.astype(BF16)

    g_in = [Gather(0, h) for h in range(2)]
    g_up = [Gather(1, h) for h in range(2)]

    def each(movers, step, *args):
        for m in movers:
            getattr(m, step)(*args)

    half_units = UNITS // 2
    chunks = [
        (1 - doubled, 0, UNITS, 0, single, 0),
        (doubled, 0, half_units, single, 2 * single, UNITS * single),
        (doubled, half_units, half_units, single, 2 * single, 2 * UNITS * single),
    ]
    rows = UNITS * single
    tiles = column_tiles(width, 256)
    full_tiles = width // 256

    def over_tiles(body):
        def step(i, carry):
            body(pl.multiple_of(i * 256, 256), 256)
            return carry

        lax.fori_loop(0, full_tiles, step, 0)
        if width % 256:
            body(full_tiles * 256, width % 256)

    def block(ref, chunk, kind, c0=None, cn=None):
        _, u0, un, r0, rn, _ = chunk
        cols = slice(None) if c0 is None else pl.ds(c0, cn)
        return ref[pl.ds(u0, un), pl.ds(kind * kind_rows + r0, rn), cols].reshape(un * rn, width if c0 is None else cn)

    def put(ref, chunk, kind, c0, cn, value):
        _, u0, un, r0, rn, _ = chunk
        ref[pl.ds(u0, un), pl.ds(kind * kind_rows + r0, rn), pl.ds(c0, cn)] = value.reshape(un, rn, cn)

    def forward_hidden(chunk):
        e, at = chunk[0], chunk[5]
        for q in range(2):
            v = jnp.dot(block(xr, chunk, 0), wi[q, e], preferred_element_type=F32)
            square = v * v
            t = jnp.tanh(gelu_scale * (v + 0.044715 * square * v))
            hid[pl.ds(at, rows), q * hidden:(q + 1) * hidden] = (0.5 * v * (1.0 + t)).astype(BF16)
            dgelu[pl.ds(at, rows), q * hidden:(q + 1) * hidden] = 0.5 * (1.0 + t) + 0.5 * v * (1.0 - t * t) * (
                gelu_scale * (1.0 + 3 * 0.044715 * square)
            )

    def forward_out(chunk):
        e, at = chunk[0], chunk[5]

        def tile(c0, cn):
            total = jnp.dot(hid[pl.ds(at, rows), 0:hidden], wo[0, e, :, pl.ds(c0, cn)], preferred_element_type=F32)
            total += jnp.dot(hid[pl.ds(at, rows), hidden:2 * hidden], wo[1, e, :, pl.ds(c0, cn)], preferred_element_type=F32)
            put(part, chunk, 1, c0, cn, total.astype(BF16))

        over_tiles(tile)

    def backward_slope(chunk):
        e, at = chunk[0], chunk[5]
        for q in range(2):
            back = lax.dot_general(block(xr, chunk, 1), wo[q, e], (((1,), (1,)), ((), ())), preferred_element_type=F32)
            slope_v[pl.ds(at, rows), q * hidden:(q + 1) * hidden] = (
                back * dgelu[pl.ds(at, rows), q * hidden:(q + 1) * hidden]
            ).astype(BF16)

    def backward_input(chunk):
        e, at = chunk[0], chunk[5]

        def tile(c0, cn):
            total = sum(
                lax.dot_general(
                    slope_v[pl.ds(at, rows), q * hidden:(q + 1) * hidden], wi[q, e, pl.ds(c0, cn), :],
                    (((1,), (1,)), ((), ())), preferred_element_type=F32,
                )
                for q in range(2)
            )
            put(part, chunk, 0, c0, cn, total.astype(BF16))

        over_tiles(tile)

    class Scatter:
        def __init__(self, k, h):
            self.k, self.h = k, h
            self.a, self.b, self.c0, self.cn = halves(h)

        def ref(self, u, r0=0, rn=None):
            rn = kind_rows if rn is None else rn
            return part.at[u, pl.ds(self.k * kind_rows + r0, rn), pl.ds(self.c0, self.cn)]

        def buf(self, slot, r0=0, rn=None):
            rn = kind_rows if rn is None else rn
            return rbuf.at[self.k, slot, pl.ds(r0, rn), pl.ds(self.c0, self.cn)]

        def unit(self, db, da):
            return unit_of(self.h, step_of(self.b, db), step_of(self.a, da))

        def send(self, u, db, da, slot, ident, rows=(0, None)):
            pltpu.make_async_remote_copy(
                src_ref=self.ref(u, *rows), dst_ref=self.buf(slot, *rows), send_sem=rs_send,
                recv_sem=rs_recv.at[self.k, self.h, ident],
                device_id={"et": self.unit(db, da)}, device_id_type=MESH,
            ).start()

        def wait(self, slot, ident, rows=(0, None)):
            ref = self.buf(slot, *rows)
            pltpu.make_async_copy(ref, ref, rs_recv.at[self.k, self.h, ident]).wait()

        def add(self, u, slots, rows=(0, None)):
            ref = self.ref(u, *rows)
            total = ref[...].astype(F32)
            for s in slots:
                total += self.buf(s, *rows)[...].astype(F32)
            ref[...] = total.astype(BF16)

        def start(self):
            for j, d in enumerate(DELTAS):
                self.send(self.unit(2, d), 1 if j < 2 else -1, 0, j, j)
            for j, d in enumerate(DELTAS):
                if j < 2:
                    self.send(self.unit(-1, d), -1, 0, 8 + j, 8 + j)
                else:
                    self.send(self.unit(1, d), 1, 0, 4 + j, 4 + j)

        def near(self, j):
            side = 1 if j < 2 else -1
            u = self.unit(side, DELTAS[j])
            self.wait(j, j)
            self.add(u, (j,))
            ident = (4 if j < 2 else 8) + j
            self.send(u, side, 0, ident, ident)

        def cross(self, j):
            u = self.unit(0, DELTAS[j])
            self.wait(4 + j, 4 + j)
            self.wait(8 + j, 8 + j)
            self.add(u, (4 + j, 8 + j))
            if j == 3:
                self.send(u, 0, 1, 12, 12, part_rows(self.k, 0))
                self.send(u, 0, -1, 12, 13, part_rows(self.k, 1))

        def far(self):
            for p, side in ((0, 1), (1, -1)):
                u = self.unit(0, side)
                piece = part_rows(self.k, p)
                self.wait(12, 12 + p, piece)
                self.add(u, (12,), piece)
                self.send(u, 0, side, 13 + p, 14 + p)

        def last(self):
            self.wait(13, 14)
            self.wait(14, 15)
            total = self.ref(self.unit(0, 0))[...].astype(F32)
            for s in (13, 14):
                total += self.buf(s)[...].astype(F32)
            own[pl.ds(self.k * kind_rows, kind_rows), pl.ds(self.c0, self.cn)] = total.astype(BF16)

    s_in = [Scatter(0, h) for h in range(2)]
    s_out = [Scatter(1, h) for h in range(2)]
    first_doubled = doubled == 0

    def tn(lhs, rhs):
        return lax.dot_general(lhs, rhs, (((0,), (0,)), ((), ())), preferred_element_type=F32)

    def whole(kind, role, c0, cn):
        r0, rn = (0, single) if role == 0 else (single, 2 * single)
        return xr[:, pl.ds(kind * kind_rows + r0, rn), pl.ds(c0, cn)].reshape(UNITS * rn, cn)

    def role_rows(ref, role):
        return ref[0:rows, :] if role == 0 else ref[rows:3 * rows, :]

    def gi_tile(c0, cn):
        by_role = [tn(whole(0, role, c0, cn), role_rows(slope_v, role)) for role in range(2)]
        for e in range(2):
            value = jnp.where(first_doubled, by_role[1 - e], by_role[e]).astype(BF16)
            for q in range(2):
                gi_v[q, e, pl.ds(c0, cn), :] = value[:, q * hidden:(q + 1) * hidden]

    def go_tile(c0, cn):
        by_role = [tn(role_rows(hid, role), whole(1, role, c0, cn)) for role in range(2)]
        for e in range(2):
            value = jnp.where(first_doubled, by_role[1 - e], by_role[e]).astype(BF16)
            for q in range(2):
                go_v[q, e, :, pl.ds(c0, cn)] = value[q * hidden:(q + 1) * hidden, :]

    def give(i, v, own_hbm, got_hbm):
        store = pltpu.make_async_copy(v.at[0], own_hbm, g_store.at[i])
        swap = pltpu.make_async_remote_copy(
            src_ref=v.at[1], dst_ref=got_hbm, send_sem=g_send.at[i], recv_sem=g_recv.at[i],
            device_id={"dp": other}, device_id_type=MESH,
        )
        store.start()
        swap.start()
        return store, swap

    def go_back(kind):
        own_rows = own[pl.ds(kind * kind_rows, kind_rows), :]
        frames_back[kind] = tn(pack_ref[...], own_rows).astype(BF16).reshape(groups, FRAME, width)
        z_exchange(kind, frames_back, zback, zb_send, zb_recv)

    def came_back(kind):
        z_arrived(kind, frames_back, zback, zb_send, zb_recv)
        return zback[kind].reshape(groups * FRAME, width)

    z_arrived(0, frames, zin, z_send, z_recv)
    unpack(0)
    each(g_in, "start")
    z_exchange(1, frames, zin, z_send, z_recv)
    for c in swaps:
        c.start()
    each(g_in, "near")
    z_arrived(1, frames, zin, z_send, z_recv)
    unpack(1)
    each(g_in, "far")
    each(g_up, "start")
    for j in range(4):
        each(g_in, "cross", j)
    each(g_up, "near")
    for c in loads:
        c.wait()
    for c in swaps:
        c.wait()
    each(g_in, "last")
    each(g_up, "far")
    forward_hidden(chunks[0])
    each(g_up, "cross", 0)
    forward_hidden(chunks[1])
    each(g_up, "cross", 1)
    forward_hidden(chunks[2])
    each(g_up, "cross", 2)
    each(g_up, "cross", 3)
    for c in chunks:
        forward_out(c)
    each(s_out, "start")
    each(g_up, "last")
    for j, c in enumerate(chunks):
        backward_slope(c)
    for j in (0, 2, 1, 3):
        each(s_out, "near", j)
    for c in chunks:
        backward_input(c)
    each(s_in, "start")
    each(s_out, "cross", 3)
    each(s_out, "cross", 1)
    over_tiles(go_tile)
    given = [give(0, go_v, go_own_hbm, go_got_hbm)]
    each(s_out, "cross", 2)
    each(s_out, "cross", 0)
    each(s_out, "far")
    for j in (0, 2, 1, 3):
        each(s_in, "near", j)
    each(s_out, "last")
    go_back(1)
    over_tiles(gi_tile)
    given.append(give(1, gi_v, gi_own_hbm, gi_got_hbm))
    for j in (3, 1, 2, 0):
        each(s_in, "cross", j)
    each(s_in, "far")
    back = came_back(1)
    first, second = tn(chosen[0], back), tn(chosen[1], back)
    layer_ref[...] = (gates[0] * first + gates[1] * second).astype(BF16)
    ggate_ref[0:1, :] = lying(jnp.sum(cot * first, axis=1, keepdims=True))
    ggate_ref[1:2, :] = lying(jnp.sum(cot * second, axis=1, keepdims=True))
    each(s_in, "last")
    go_back(0)
    gtok_ref[...] = tn(either, came_back(0)).astype(BF16)

    sent = xr.at[pl.ds(0, UNITS - 1)]
    pltpu.make_async_copy(sent, sent, ag_send).wait()
    sent = part.at[pl.ds(0, UNITS - 1)]
    pltpu.make_async_copy(sent, sent, rs_send).wait()
    for store, swap in given:
        store.wait()
        swap.wait()


def shards(mesh_shape, tokens, gate_probs, expert_ids, copies, weight_in, weight_out, cotangent):
    groups = mesh_shape["ex"]
    count, width = tokens.shape
    hidden = weight_in.shape[2]
    unit_rows = 12 * groups
    kind_rows = 6 * groups
    all_rows = UNITS * kind_rows
    pack = jnp.asarray(pack_matrix(groups), BF16)
    vmem, anywhere = pl.BlockSpec(memory_space=pltpu.VMEM), pl.BlockSpec(memory_space=pl.ANY)
    shape = jax.ShapeDtypeStruct
    dma = pltpu.SemaphoreType.DMA
    results = pl.pallas_call(
        functools.partial(layer_kernel, groups),
        out_shape=(
            shape((count, width), BF16), shape((count, width), BF16), shape((2, count), F32),
            shape(weight_in.shape, BF16), shape(weight_in.shape, BF16),
            shape(weight_out.shape, BF16), shape(weight_out.shape, BF16),
        ),
        in_specs=[pl.BlockSpec(memory_space=pltpu.HBM)] * 8,
        out_specs=(vmem, vmem, vmem, anywhere, anywhere, anywhere, anywhere),
        scratch_shapes=[
            pltpu.VMEM((2, count), jnp.int32), pltpu.SMEM(copies.shape, jnp.int32), pltpu.VMEM(pack.shape, BF16),
            pltpu.VMEM((count, width), BF16), pltpu.VMEM((count, width), BF16), pltpu.VMEM((2, count), F32),
            pltpu.VMEM((2,) + weight_in.shape, BF16),
            pltpu.VMEM((2,) + weight_out.shape, BF16),
            pltpu.VMEM((2, groups, FRAME, width), BF16),
            pltpu.VMEM((2, groups, FRAME, width), BF16),
            pltpu.VMEM((UNITS, unit_rows, width), BF16),
            pltpu.VMEM((UNITS, unit_rows, width), BF16),
            pltpu.VMEM((2, 15, kind_rows, width), BF16),
            pltpu.VMEM((unit_rows, width), BF16),
            pltpu.VMEM((2, groups, FRAME, width), BF16),
            pltpu.VMEM((2, groups, FRAME, width), BF16),
            pltpu.VMEM((all_rows, 2 * hidden), BF16),
            pltpu.VMEM((all_rows, 2 * hidden), BF16),
            pltpu.VMEM((all_rows, 2 * hidden), F32),
            pltpu.VMEM((2,) + weight_in.shape, BF16),
            pltpu.VMEM((2,) + weight_out.shape, BF16),
            dma((6,)), dma((2,)), dma((2,)), dma((2,)),
            dma((2,)), dma((2, groups)),
            dma(()), dma((2, 2, 16)),
            dma(()), dma((2, 2, 16)),
            dma((2,)), dma((2, groups)),
            dma((2,)), dma((2,)), dma((2,)),
        ],
        compiler_params=pltpu.CompilerParams(
            collective_id=0, has_side_effects=True, vmem_limit_bytes=46 * 2**20
        ),
        name="moe_layer",
    )(*(
        pltpu.with_memory_space_constraint(v, pltpu.HBM)
        for v in (expert_ids.T, copies, pack, tokens, cotangent, gate_probs.T, weight_in, weight_out)
    ))
    layer_out, grad_tokens, grad_gates, gi_own, gi_got, go_own, go_got = results
    return (
        layer_out,
        grad_tokens,
        grad_gates.T,
        gi_own.astype(F32) + gi_got.astype(F32),
        go_own.astype(F32) + go_got.astype(F32),
    )


def solution(mesh):
    rows = P(("et", "ex", "dp"), None)
    w_in = P("ex", None, ("et", "dp"))
    w_out = P("ex", ("et", "dp"), None)
    return jax.shard_map(
        functools.partial(shards, dict(mesh.shape)),
        mesh=mesh,
        in_specs=(rows, rows, rows, P(), w_in, w_out, rows),
        out_specs=(rows, rows, rows, w_in, w_out),
        check_vma=False,
    )
```

```python
import functools

import jax
import jax.numpy as jnp
import numpy as np
from jax import lax
from jax.experimental import pallas as pl
from jax.experimental.pallas import tpu as pltpu
from jax.sharding import PartitionSpec as P

MESH = pl.DeviceIdType.MESH
SIDE = 4
UNITS = SIDE * SIDE
FRAME = 8
DELTAS = (0, -1, 1, 2)
F32 = jnp.float32
BF16 = jnp.bfloat16
gelu_scale = 0.7978845608028654


def pack_matrix(groups):
    single = 2 * groups
    out = np.zeros((3 * single, groups * FRAME), np.float32)
    for r in range(single):
        out[r, (r // 2) * FRAME + r % 2] = 1
    for r in range(2 * single):
        out[single + r, (r // 4) * FRAME + 2 + r % 4] = 1
    return out


def column_tiles(width, step):
    return [(c, min(step, width - c)) for c in range(0, width, step)]


def layer_kernel(
    groups, ids_hbm, copies_hbm, pack_hbm, tokens_hbm, cot_hbm, gates_hbm, wi_hbm, wo_hbm,
    layer_ref, gtok_ref, ggate_ref, gi_own_hbm, gi_got_hbm, go_own_hbm, go_got_hbm,
    ids_ref, copies_ref, pack_ref, tokens_ref, cot_ref, gates_ref, wi, wo, frames, zin, xr, part, rbuf, own, frames_back, zback, hid, slope_v, dgelu, gi_v, go_v,
    in_load, w_send, w_recv, w_load, z_send, z_recv, ag_send, ag_recv, rs_send, rs_recv, zb_send, zb_recv, g_send, g_recv, g_store,
):
    width = tokens_ref.shape[1]
    hidden = wi.shape[3]
    et = lax.axis_index("et")
    ex = lax.axis_index("ex")
    dp = lax.axis_index("dp")
    y, x = lax.div(et, SIDE), lax.rem(et, SIDE)
    other = 1 - dp
    kind_rows = 6 * groups
    single = 2 * groups
    half_cut = (width // 128 + 1) // 2 * 128

    def step_of(v, d):
        return lax.rem(v + (d + SIDE), SIDE)

    def unit_of(h, b, a):
        return b * SIDE + a if h == 0 else a * SIDE + b

    arrays = [
        pltpu.make_async_copy(hbm, v, in_load.at[i])
        for i, (hbm, v) in enumerate((
            (ids_hbm, ids_ref), (copies_hbm, copies_ref), (gates_hbm, gates_ref),
            (cot_hbm, cot_ref), (tokens_hbm, tokens_ref), (pack_hbm, pack_ref),
        ))
    ]
    for c in arrays:
        c.start()

    barrier = pltpu.get_barrier_semaphore()
    for dev in (
        unit_of(0, y, step_of(x, 1)), unit_of(0, y, step_of(x, -1)),
        unit_of(0, step_of(y, 1), x), unit_of(0, step_of(y, -1), x),
    ):
        pl.semaphore_signal(barrier, inc=1, device_id={"et": dev}, device_id_type=MESH)
    for o in range(1, groups):
        pl.semaphore_signal(barrier, inc=1, device_id={"ex": lax.rem(ex + o, groups)}, device_id_type=MESH)
    pl.semaphore_signal(barrier, inc=1, device_id={"dp": other}, device_id_type=MESH)

    loads = [
        pltpu.make_async_copy(wi_hbm, wi.at[0], w_load.at[0]),
        pltpu.make_async_copy(wo_hbm, wo.at[0], w_load.at[1]),
    ]
    for c in loads:
        c.start()

    for c in arrays:
        c.wait()
    doubled = jnp.where(copies_ref[2 * ex + 1] == 2, 1, 0)
    count = tokens_ref.shape[0]
    square = (count, count)
    down, along = lax.broadcasted_iota(jnp.int32, square, 0), lax.broadcasted_iota(jnp.int32, square, 1)
    diagonal = down == along

    def upright(row):
        return jnp.sum(jnp.where(diagonal, jnp.broadcast_to(row, square), 0.0), axis=1, keepdims=True)

    def lying(column):
        return jnp.sum(jnp.where(diagonal, jnp.broadcast_to(column, square), 0.0), axis=0, keepdims=True)

    ids = [ids_ref[k:k + 1, :] for k in range(2)]
    columns = [upright(v.astype(F32)) for v in ids]
    spots = lax.broadcasted_iota(jnp.int32, (groups * FRAME, count), 0)
    chosen = []
    for k in range(2):
        mine = ids[k].astype(F32)
        same = sum(jnp.where((c == mine) & (down < along), 1.0, 0.0) for c in columns)
        rank = jnp.sum(same, axis=0, keepdims=True).astype(jnp.int32)
        held = jnp.zeros_like(ids[k])
        for e in range(2 * groups):
            held = jnp.where(ids[k] == e, copies_ref[e], held)
        spot = (ids[k] >> 1) * FRAME + jnp.where(held == 2, 2 + rank, rank)
        spot = jnp.where(rank < 2 * held, spot, -1)
        chosen.append(jnp.where(spots == spot, 1.0, 0.0).astype(BF16))
    either = chosen[0] + chosen[1]
    gates = [upright(gates_ref[k:k + 1, :]) for k in range(2)]
    cot = cot_ref[...].astype(F32)

    def fill(kind, value):
        frames[kind] = value.astype(BF16).reshape(groups, FRAME, width)

    fill(0, jnp.dot(either, tokens_ref[...], preferred_element_type=F32))
    fill(1, sum(jnp.dot(c, (cot * g).astype(BF16), preferred_element_type=F32) for c, g in zip(chosen, gates)))

    pl.semaphore_wait(barrier, 4 + groups - 1 + 1)

    spans = ((0, half_cut), (half_cut, width - half_cut))

    def z_exchange(kind, h, src, dst, send, recv):
        cols = pl.ds(*spans[h])
        for o in range(1, groups):
            peer = lax.rem(ex + o, groups)
            pltpu.make_async_remote_copy(
                src_ref=src.at[kind, peer, :, cols], dst_ref=dst.at[kind, ex, :, cols],
                send_sem=send.at[kind, h], recv_sem=recv.at[kind, h, ex],
                device_id={"ex": peer}, device_id_type=MESH,
            ).start()
        dst[kind, ex, :, cols] = src[kind, ex, :, cols]

    def z_arrived(kind, h, src, dst, send, recv):
        cols = pl.ds(*spans[h])
        for o in range(1, groups):
            peer = lax.rem(ex + o, groups)
            pltpu.make_async_copy(src.at[kind, peer, :, cols], dst.at[kind, peer, :, cols], recv.at[kind, h, peer]).wait()
        sent = src.at[kind, pl.ds(0, groups - 1), :, cols]
        pltpu.make_async_copy(sent, sent, send.at[kind, h]).wait()

    for h in range(2):
        z_exchange(0, h, frames, zin, z_send, z_recv)
    swaps = [
        pltpu.make_async_remote_copy(
            src_ref=hbm, dst_ref=v.at[1], send_sem=w_send.at[i], recv_sem=w_recv.at[i],
            device_id={"dp": other}, device_id_type=MESH,
        )
        for i, (hbm, v) in enumerate(((wi_hbm, wi), (wo_hbm, wo)))
    ]

    def halves(k, h):
        a, b = (x, y) if h == k else (y, x)
        return (a, b) + spans[h]

    def part_rows(k, p):
        cut = single if k == 0 else 2 * single
        return (0, cut) if p == 0 else (cut, kind_rows - cut)

    class Gather:
        def __init__(self, k, h):
            self.k, self.h = k, h
            self.a, self.b, self.c0, self.cn = halves(k, h)

        def ref(self, u, r0=0, rn=None):
            rn = kind_rows if rn is None else rn
            return xr.at[u, pl.ds(self.k * kind_rows + r0, rn), pl.ds(self.c0, self.cn)]

        def unit(self, db, da):
            return unit_of(self.h ^ self.k, step_of(self.b, db), step_of(self.a, da))

        def send(self, u, db, da, ident, rows=(0, None)):
            ref = self.ref(u, *rows)
            pltpu.make_async_remote_copy(
                src_ref=ref, dst_ref=ref, send_sem=ag_send, recv_sem=ag_recv.at[self.k, self.h, ident],
                device_id={"et": self.unit(db, da)}, device_id_type=MESH,
            ).start()

        def wait(self, u, ident, rows=(0, None)):
            ref = self.ref(u, *rows)
            pltpu.make_async_copy(ref, ref, ag_recv.at[self.k, self.h, ident]).wait()

        def start(self):
            u = self.unit(0, 0)
            self.send(u, 0, 1, 0)
            self.send(u, 0, -1, 1)
            self.send(u, 1, 0, 4)
            self.send(u, -1, 0, 8)

        def near(self):
            u = self.unit(0, -1)
            self.wait(u, 0)
            self.send(u, 0, 1, 2, part_rows(self.k, 0))
            self.send(u, 1, 0, 5)
            self.send(u, -1, 0, 9)
            u = self.unit(0, 1)
            self.wait(u, 1)
            self.send(u, 0, -1, 3, part_rows(self.k, 1))
            self.send(u, 1, 0, 6)
            self.send(u, -1, 0, 10)

        def far(self):
            u = self.unit(0, 2)
            self.wait(u, 2, part_rows(self.k, 0))
            self.wait(u, 3, part_rows(self.k, 1))
            self.send(u, 1, 0, 7)
            self.send(u, -1, 0, 11)

        def cross(self, j):
            d = DELTAS[j]
            u = self.unit(-1, d)
            self.wait(u, 4 + j)
            if j < 2:
                self.send(u, 1, 0, 12 + j)
            u = self.unit(1, d)
            self.wait(u, 8 + j)
            if j >= 2:
                self.send(u, -1, 0, 12 + j)

        def last(self):
            for j, d in enumerate(DELTAS):
                self.wait(self.unit(2, d), 12 + j)

    def unpack(kind, h):
        cols = pl.ds(*spans[h])
        z_arrived(kind, h, frames, zin, z_send, z_recv)
        frame_rows = zin[kind, :, :, cols].reshape(groups * FRAME, spans[h][1])
        unit_rows = jnp.dot(pack_ref[...], frame_rows, preferred_element_type=F32)
        xr[et, pl.ds(kind * kind_rows, kind_rows), cols] = unit_rows.astype(BF16)

    g_in = [Gather(0, h) for h in range(2)]
    g_up = [Gather(1, h) for h in range(2)]

    def each(movers, step, *args):
        for m in movers:
            getattr(m, step)(*args)

    half_units = UNITS // 2
    chunks = [
        (1 - doubled, 0, UNITS, 0, single, 0),
        (doubled, 0, half_units, single, 2 * single, UNITS * single),
        (doubled, half_units, half_units, single, 2 * single, 2 * UNITS * single),
    ]
    rows = UNITS * single
    tiles = column_tiles(width, 256)
    full_tiles = width // 256

    def over_tiles(body):
        def step(i, carry):
            body(pl.multiple_of(i * 256, 256), 256)
            return carry

        lax.fori_loop(0, full_tiles, step, 0)
        if width % 256:
            body(full_tiles * 256, width % 256)

    def block(ref, chunk, kind, c0=None, cn=None):
        _, u0, un, r0, rn, _ = chunk
        cols = slice(None) if c0 is None else pl.ds(c0, cn)
        return ref[pl.ds(u0, un), pl.ds(kind * kind_rows + r0, rn), cols].reshape(un * rn, width if c0 is None else cn)

    def put(ref, chunk, kind, c0, cn, value):
        _, u0, un, r0, rn, _ = chunk
        ref[pl.ds(u0, un), pl.ds(kind * kind_rows + r0, rn), pl.ds(c0, cn)] = value.reshape(un, rn, cn)

    def forward_hidden(chunk):
        e, at = chunk[0], chunk[5]
        for q in range(2):
            v = jnp.dot(block(xr, chunk, 0), wi[q, e], preferred_element_type=F32)
            square = v * v
            t = jnp.tanh(gelu_scale * (v + 0.044715 * square * v))
            hid[pl.ds(at, rows), q * hidden:(q + 1) * hidden] = (0.5 * v * (1.0 + t)).astype(BF16)
            dgelu[pl.ds(at, rows), q * hidden:(q + 1) * hidden] = 0.5 * (1.0 + t) + 0.5 * v * (1.0 - t * t) * (
                gelu_scale * (1.0 + 3 * 0.044715 * square)
            )

    def forward_out(chunk):
        e, at = chunk[0], chunk[5]

        def tile(c0, cn):
            total = jnp.dot(hid[pl.ds(at, rows), 0:hidden], wo[0, e, :, pl.ds(c0, cn)], preferred_element_type=F32)
            total += jnp.dot(hid[pl.ds(at, rows), hidden:2 * hidden], wo[1, e, :, pl.ds(c0, cn)], preferred_element_type=F32)
            put(part, chunk, 1, c0, cn, total.astype(BF16))

        over_tiles(tile)

    def backward_slope(chunk):
        e, at = chunk[0], chunk[5]
        for q in range(2):
            back = lax.dot_general(block(xr, chunk, 1), wo[q, e], (((1,), (1,)), ((), ())), preferred_element_type=F32)
            slope_v[pl.ds(at, rows), q * hidden:(q + 1) * hidden] = (
                back * dgelu[pl.ds(at, rows), q * hidden:(q + 1) * hidden]
            ).astype(BF16)

    def backward_input(chunk):
        e, at = chunk[0], chunk[5]

        def tile(c0, cn):
            total = sum(
                lax.dot_general(
                    slope_v[pl.ds(at, rows), q * hidden:(q + 1) * hidden], wi[q, e, pl.ds(c0, cn), :],
                    (((1,), (1,)), ((), ())), preferred_element_type=F32,
                )
                for q in range(2)
            )
            put(part, chunk, 0, c0, cn, total.astype(BF16))

        over_tiles(tile)

    class Scatter:
        def __init__(self, k, h):
            self.k, self.h = k, h
            self.a, self.b, self.c0, self.cn = halves(k, h)

        def ref(self, u, r0=0, rn=None):
            rn = kind_rows if rn is None else rn
            return part.at[u, pl.ds(self.k * kind_rows + r0, rn), pl.ds(self.c0, self.cn)]

        def buf(self, slot, r0=0, rn=None):
            rn = kind_rows if rn is None else rn
            return rbuf.at[self.k, slot, pl.ds(r0, rn), pl.ds(self.c0, self.cn)]

        def unit(self, db, da):
            return unit_of(self.h ^ self.k, step_of(self.b, db), step_of(self.a, da))

        def send(self, u, db, da, slot, ident, rows=(0, None)):
            pltpu.make_async_remote_copy(
                src_ref=self.ref(u, *rows), dst_ref=self.buf(slot, *rows), send_sem=rs_send,
                recv_sem=rs_recv.at[self.k, self.h, ident],
                device_id={"et": self.unit(db, da)}, device_id_type=MESH,
            ).start()

        def wait(self, slot, ident, rows=(0, None)):
            ref = self.buf(slot, *rows)
            pltpu.make_async_copy(ref, ref, rs_recv.at[self.k, self.h, ident]).wait()

        def add(self, u, slots, rows=(0, None)):
            ref = self.ref(u, *rows)
            total = ref[...].astype(F32)
            for s in slots:
                total += self.buf(s, *rows)[...].astype(F32)
            ref[...] = total.astype(BF16)

        def start(self):
            order = (3, 1, 2, 0)
            for j in order:
                self.send(self.unit(2, DELTAS[j]), 1 if j < 2 else -1, 0, j, j)
            for j in order:
                d = DELTAS[j]
                if j < 2:
                    self.send(self.unit(-1, d), -1, 0, 8 + j, 8 + j)
                else:
                    self.send(self.unit(1, d), 1, 0, 4 + j, 4 + j)

        def near(self, j):
            side = 1 if j < 2 else -1
            u = self.unit(side, DELTAS[j])
            self.wait(j, j)
            self.add(u, (j,))
            ident = (4 if j < 2 else 8) + j
            self.send(u, side, 0, ident, ident)

        def cross(self, j):
            u = self.unit(0, DELTAS[j])
            self.wait(4 + j, 4 + j)
            self.wait(8 + j, 8 + j)
            self.add(u, (4 + j, 8 + j))
            if j == 3:
                self.send(u, 0, 1, 12, 12, part_rows(self.k, 0))
                self.send(u, 0, -1, 12, 13, part_rows(self.k, 1))

        def far(self):
            for p, side in ((0, 1), (1, -1)):
                u = self.unit(0, side)
                piece = part_rows(self.k, p)
                self.wait(12, 12 + p, piece)
                self.add(u, (12,), piece)
                self.send(u, 0, side, 13 + p, 14 + p)

        def last(self):
            self.wait(13, 14)
            self.wait(14, 15)
            total = self.ref(self.unit(0, 0))[...].astype(F32)
            for s in (13, 14):
                total += self.buf(s)[...].astype(F32)
            own[pl.ds(self.k * kind_rows, kind_rows), pl.ds(self.c0, self.cn)] = total.astype(BF16)

    s_in = [Scatter(0, h) for h in range(2)]
    s_out = [Scatter(1, h) for h in range(2)]
    first_doubled = doubled == 0

    def tn(lhs, rhs):
        return lax.dot_general(lhs, rhs, (((0,), (0,)), ((), ())), preferred_element_type=F32)

    def whole(kind, role, c0, cn):
        r0, rn = (0, single) if role == 0 else (single, 2 * single)
        return xr[:, pl.ds(kind * kind_rows + r0, rn), pl.ds(c0, cn)].reshape(UNITS * rn, cn)

    def role_rows(ref, role):
        return ref[0:rows, :] if role == 0 else ref[rows:3 * rows, :]

    def gi_tile(c0, cn):
        by_role = [tn(whole(0, role, c0, cn), role_rows(slope_v, role)) for role in range(2)]
        for e in range(2):
            value = jnp.where(first_doubled, by_role[1 - e], by_role[e]).astype(BF16)
            for q in range(2):
                gi_v[q, e, pl.ds(c0, cn), :] = value[:, q * hidden:(q + 1) * hidden]

    def go_tile(c0, cn):
        by_role = [tn(role_rows(hid, role), whole(1, role, c0, cn)) for role in range(2)]
        for e in range(2):
            value = jnp.where(first_doubled, by_role[1 - e], by_role[e]).astype(BF16)
            for q in range(2):
                go_v[q, e, :, pl.ds(c0, cn)] = value[q * hidden:(q + 1) * hidden, :]

    def give(i, v, own_hbm, got_hbm):
        store = pltpu.make_async_copy(v.at[0], own_hbm, g_store.at[i])
        swap = pltpu.make_async_remote_copy(
            src_ref=v.at[1], dst_ref=got_hbm, send_sem=g_send.at[i], recv_sem=g_recv.at[i],
            device_id={"dp": other}, device_id_type=MESH,
        )
        store.start()
        swap.start()
        return store, swap

    def go_back(kind, h):
        cols = pl.ds(*spans[h])
        own_rows = own[pl.ds(kind * kind_rows, kind_rows), cols]
        frames_back[kind, :, :, cols] = tn(pack_ref[...], own_rows).astype(BF16).reshape(groups, FRAME, spans[h][1])
        z_exchange(kind, h, frames_back, zback, zb_send, zb_recv)

    def came_back(kind, h):
        z_arrived(kind, h, frames_back, zback, zb_send, zb_recv)
        return zback[kind, :, :, pl.ds(*spans[h])].reshape(groups * FRAME, spans[h][1])

    def finish_out():
        dots = [0.0, 0.0]
        for h in range(2):
            cols = pl.ds(*spans[h])
            back = came_back(1, h)
            pair = [tn(c, back) for c in chosen]
            layer_ref[:, cols] = (gates[0] * pair[0] + gates[1] * pair[1]).astype(BF16)
            part_cot = cot_ref[:, cols].astype(F32)
            dots = [d + jnp.sum(part_cot * p, axis=1, keepdims=True) for d, p in zip(dots, pair)]
        for k in range(2):
            ggate_ref[k:k + 1, :] = lying(dots[k])

    unpack(0, 0)
    g_in[0].start()
    unpack(0, 1)
    g_in[1].start()
    for h in range(2):
        z_exchange(1, h, frames, zin, z_send, z_recv)
    for c in swaps:
        c.start()
    each(g_in, "near")
    each(g_in, "far")
    each(g_in, "cross", 0)
    each(g_in, "cross", 1)
    for h in range(2):
        unpack(1, h)
        g_up[h].start()
    each(g_in, "cross", 2)
    each(g_in, "cross", 3)
    for c in loads:
        c.wait()
    for c in swaps:
        c.wait()
    each(g_in, "last")
    each(g_up, "near")
    forward_hidden(chunks[0])
    each(g_up, "far")
    forward_hidden(chunks[1])
    forward_hidden(chunks[2])
    each(g_up, "cross", 0)
    forward_out(chunks[0])
    each(g_up, "cross", 1)
    forward_out(chunks[1])
    each(g_up, "cross", 2)
    forward_out(chunks[2])
    each(g_up, "cross", 3)
    each(s_out, "start")
    each(g_up, "last")
    backward_slope(chunks[0])
    backward_slope(chunks[1])
    each(s_out, "near", 3)
    each(s_out, "near", 1)
    backward_slope(chunks[2])
    each(s_out, "near", 2)
    each(s_out, "near", 0)
    backward_input(chunks[0])
    backward_input(chunks[1])
    each(s_out, "cross", 3)
    backward_input(chunks[2])
    each(s_in, "start")
    each(s_out, "cross", 1)
    each(s_out, "cross", 2)
    each(s_out, "far")
    each(s_in, "near", 3)
    each(s_in, "near", 1)
    over_tiles(go_tile)
    given = [give(0, go_v, go_own_hbm, go_got_hbm)]
    each(s_out, "cross", 0)
    each(s_in, "near", 2)
    each(s_in, "near", 0)
    for h in range(2):
        s_out[h].last()
        go_back(1, h)
    each(s_in, "cross", 3)
    each(s_in, "cross", 1)
    each(s_in, "cross", 2)
    each(s_in, "far")
    over_tiles(gi_tile)
    given.append(give(1, gi_v, gi_own_hbm, gi_got_hbm))
    each(s_in, "cross", 0)
    finish_out()
    for h in range(2):
        s_in[h].last()
        go_back(0, h)
    for h in range(2):
        gtok_ref[:, pl.ds(*spans[h])] = tn(either, came_back(0, h)).astype(BF16)

    sent = xr.at[pl.ds(0, UNITS - 1)]
    pltpu.make_async_copy(sent, sent, ag_send).wait()
    sent = part.at[pl.ds(0, UNITS - 1)]
    pltpu.make_async_copy(sent, sent, rs_send).wait()
    for store, swap in given:
        store.wait()
        swap.wait()


def finish_kernel(
    layer_ref, gtok_ref, ggate_ref, gi_own, gi_got, go_own, go_got,
    layer_hbm, gtok_hbm, ggate_hbm, gi_hbm, go_hbm, gi_v, go_v, small_sem, sum_sem,
):
    copies = [
        pltpu.make_async_copy(v, hbm, small_sem.at[i])
        for i, (v, hbm) in enumerate(((layer_ref, layer_hbm), (gtok_ref, gtok_hbm), (ggate_ref, ggate_hbm)))
    ]
    for c in copies:
        c.start()
    for i, (own, got, total, hbm) in enumerate(((gi_own, gi_got, gi_v, gi_hbm), (go_own, go_got, go_v, go_hbm))):
        piece = own.shape[1] // 4
        for e in range(2):
            for n in range(4):
                here = (e, pl.ds(n * piece, piece))
                total[here] = own[here].astype(F32) + got[here].astype(F32)
                copies.append(pltpu.make_async_copy(total.at[here], hbm.at[here], sum_sem.at[i, e, n]))
                copies[-1].start()
    for c in copies:
        c.wait()


def shards(mesh_shape, tokens, gate_probs, expert_ids, copies, weight_in, weight_out, cotangent):
    groups = mesh_shape["ex"]
    count, width = tokens.shape
    hidden = weight_in.shape[2]
    unit_rows = 12 * groups
    kind_rows = 6 * groups
    all_rows = UNITS * kind_rows
    pack = jnp.asarray(pack_matrix(groups), BF16)
    vmem, anywhere = pl.BlockSpec(memory_space=pltpu.VMEM), pl.BlockSpec(memory_space=pl.ANY)
    shape = jax.ShapeDtypeStruct
    dma = pltpu.SemaphoreType.DMA
    results = pl.pallas_call(
        functools.partial(layer_kernel, groups),
        out_shape=(
            shape((count, width), BF16), shape((count, width), BF16), shape((2, count), F32),
            shape(weight_in.shape, BF16), shape(weight_in.shape, BF16),
            shape(weight_out.shape, BF16), shape(weight_out.shape, BF16),
        ),
        in_specs=[pl.BlockSpec(memory_space=pltpu.HBM)] * 8,
        out_specs=(vmem, vmem, vmem, anywhere, anywhere, anywhere, anywhere),
        scratch_shapes=[
            pltpu.VMEM((2, count), jnp.int32), pltpu.SMEM(copies.shape, jnp.int32), pltpu.VMEM(pack.shape, BF16),
            pltpu.VMEM((count, width), BF16), pltpu.VMEM((count, width), BF16), pltpu.VMEM((2, count), F32),
            pltpu.VMEM((2,) + weight_in.shape, BF16),
            pltpu.VMEM((2,) + weight_out.shape, BF16),
            pltpu.VMEM((2, groups, FRAME, width), BF16),
            pltpu.VMEM((2, groups, FRAME, width), BF16),
            pltpu.VMEM((UNITS, unit_rows, width), BF16),
            pltpu.VMEM((UNITS, unit_rows, width), BF16),
            pltpu.VMEM((2, 15, kind_rows, width), BF16),
            pltpu.VMEM((unit_rows, width), BF16),
            pltpu.VMEM((2, groups, FRAME, width), BF16),
            pltpu.VMEM((2, groups, FRAME, width), BF16),
            pltpu.VMEM((all_rows, 2 * hidden), BF16),
            pltpu.VMEM((all_rows, 2 * hidden), BF16),
            pltpu.VMEM((all_rows, 2 * hidden), F32),
            pltpu.VMEM((2,) + weight_in.shape, BF16),
            pltpu.VMEM((2,) + weight_out.shape, BF16),
            dma((6,)), dma((2,)), dma((2,)), dma((2,)),
            dma((2, 2)), dma((2, 2, groups)),
            dma(()), dma((2, 2, 16)),
            dma(()), dma((2, 2, 16)),
            dma((2, 2)), dma((2, 2, groups)),
            dma((2,)), dma((2,)), dma((2,)),
        ],
        compiler_params=pltpu.CompilerParams(
            collective_id=0, has_side_effects=True, vmem_limit_bytes=46 * 2**20
        ),
        name="moe_layer",
    )(*(
        pltpu.with_memory_space_constraint(v, pltpu.HBM)
        for v in (expert_ids.T, copies, pack, tokens, cotangent, gate_probs.T, weight_in, weight_out)
    ))
    hbm = pl.BlockSpec(memory_space=pltpu.HBM)
    layer_out, grad_tokens, grad_gates, grad_in, grad_out = pl.pallas_call(
        finish_kernel,
        out_shape=(
            shape((count, width), BF16), shape((count, width), BF16), shape((2, count), F32),
            shape(weight_in.shape, F32), shape(weight_out.shape, F32),
        ),
        in_specs=[vmem] * 7,
        out_specs=(hbm,) * 5,
        scratch_shapes=[
            pltpu.VMEM(weight_in.shape, F32), pltpu.VMEM(weight_out.shape, F32), dma((3,)), dma((2, 2, 4)),
        ],
        compiler_params=pltpu.CompilerParams(vmem_limit_bytes=8 * 2**20),
        name="replica_sums",
    )(*(pltpu.with_memory_space_constraint(v, pltpu.VMEM) for v in results))
    return layer_out, grad_tokens, grad_gates.T, grad_in, grad_out


def solution(mesh):
    rows = P(("et", "ex", "dp"), None)
    w_in = P("ex", None, ("et", "dp"))
    w_out = P("ex", ("et", "dp"), None)
    return jax.shard_map(
        functools.partial(shards, dict(mesh.shape)),
        mesh=mesh,
        in_specs=(rows, rows, rows, P(), w_in, w_out, rows),
        out_specs=(rows, rows, rows, w_in, w_out),
        check_vma=False,
    )
```

```python
import functools

import jax
import jax.numpy as jnp
import numpy as np
from jax import lax
from jax.experimental import pallas as pl
from jax.experimental.pallas import tpu as pltpu
from jax.sharding import PartitionSpec as P

MESH = pl.DeviceIdType.MESH
SIDE = 4
UNITS = SIDE * SIDE
FRAME = 8
DELTAS = (0, -1, 1, 2)
F32 = jnp.float32
BF16 = jnp.bfloat16
gelu_scale = 0.7978845608028654


def pack_matrix(groups):
    single = 2 * groups
    out = np.zeros((3 * single, groups * FRAME), np.float32)
    for r in range(single):
        out[r, (r // 2) * FRAME + r % 2] = 1
    for r in range(2 * single):
        out[single + r, (r // 4) * FRAME + 2 + r % 4] = 1
    return out


def column_tiles(width, step):
    return [(c, min(step, width - c)) for c in range(0, width, step)]


def layer_kernel(
    groups, ids_hbm, copies_hbm, pack_hbm, tokens_hbm, cot_hbm, gates_hbm, wi_hbm, wo_hbm,
    layer_ref, gtok_ref, ggate_ref, gi_own_hbm, gi_got_hbm, go_own_hbm, go_got_hbm,
    ids_ref, copies_ref, pack_ref, tokens_ref, cot_ref, gates_ref, wi, wo, frames, zin, xr, part, rbuf, own, frames_back, zback, hid, slope_v, dgelu, gi_v, go_v,
    in_load, w_send, w_recv, w_load, z_send, z_recv, ag_send, ag_recv, rs_send, rs_recv, zb_send, zb_recv, g_send, g_recv, g_store,
):
    width = tokens_ref.shape[1]
    hidden = wi.shape[3]
    et = lax.axis_index("et")
    ex = lax.axis_index("ex")
    dp = lax.axis_index("dp")
    y, x = lax.div(et, SIDE), lax.rem(et, SIDE)
    other = 1 - dp
    kind_rows = 6 * groups
    single = 2 * groups
    half_cut = (width // 128 + 1) // 2 * 128

    def step_of(v, d):
        return lax.rem(v + (d + SIDE), SIDE)

    def unit_of(h, b, a):
        return b * SIDE + a if h == 0 else a * SIDE + b

    arrays = [
        pltpu.make_async_copy(hbm, v, in_load.at[i])
        for i, (hbm, v) in enumerate((
            (ids_hbm, ids_ref), (copies_hbm, copies_ref), (gates_hbm, gates_ref),
            (cot_hbm, cot_ref), (tokens_hbm, tokens_ref), (pack_hbm, pack_ref),
        ))
    ]
    for c in arrays:
        c.start()

    barrier = pltpu.get_barrier_semaphore()
    for dev in (
        unit_of(0, y, step_of(x, 1)), unit_of(0, y, step_of(x, -1)),
        unit_of(0, step_of(y, 1), x), unit_of(0, step_of(y, -1), x),
        unit_of(0, y, step_of(x, 2)), unit_of(0, step_of(y, 2), x),
    ):
        pl.semaphore_signal(barrier, inc=1, device_id={"et": dev}, device_id_type=MESH)
    for o in range(1, groups):
        pl.semaphore_signal(barrier, inc=1, device_id={"ex": lax.rem(ex + o, groups)}, device_id_type=MESH)
    pl.semaphore_signal(barrier, inc=1, device_id={"dp": other}, device_id_type=MESH)

    loads = [
        pltpu.make_async_copy(wi_hbm, wi.at[0], w_load.at[0]),
        pltpu.make_async_copy(wo_hbm, wo.at[0], w_load.at[1]),
    ]
    for c in loads:
        c.start()

    for c in arrays:
        c.wait()
    doubled = jnp.where(copies_ref[2 * ex + 1] == 2, 1, 0)
    count = tokens_ref.shape[0]
    square = (count, count)
    down, along = lax.broadcasted_iota(jnp.int32, square, 0), lax.broadcasted_iota(jnp.int32, square, 1)
    diagonal = down == along

    def upright(row):
        return jnp.sum(jnp.where(diagonal, jnp.broadcast_to(row, square), 0.0), axis=1, keepdims=True)

    def lying(column):
        return jnp.sum(jnp.where(diagonal, jnp.broadcast_to(column, square), 0.0), axis=0, keepdims=True)

    ids = [ids_ref[k:k + 1, :] for k in range(2)]
    columns = [upright(v.astype(F32)) for v in ids]
    spots = lax.broadcasted_iota(jnp.int32, (groups * FRAME, count), 0)
    chosen = []
    for k in range(2):
        mine = ids[k].astype(F32)
        same = sum(jnp.where((c == mine) & (down < along), 1.0, 0.0) for c in columns)
        rank = jnp.sum(same, axis=0, keepdims=True).astype(jnp.int32)
        held = jnp.zeros_like(ids[k])
        for e in range(2 * groups):
            held = jnp.where(ids[k] == e, copies_ref[e], held)
        spot = (ids[k] >> 1) * FRAME + jnp.where(held == 2, 2 + rank, rank)
        spot = jnp.where(rank < 2 * held, spot, -1)
        chosen.append(jnp.where(spots == spot, 1.0, 0.0).astype(BF16))
    either = chosen[0] + chosen[1]
    gates = [upright(gates_ref[k:k + 1, :]) for k in range(2)]

    spans = ((0, half_cut), (half_cut, width - half_cut))

    def z_exchange(kind, h, src, dst, send, recv):
        cols = pl.ds(*spans[h])
        for o in range(1, groups):
            peer = lax.rem(ex + o, groups)
            pltpu.make_async_remote_copy(
                src_ref=src.at[kind, peer, :, cols], dst_ref=dst.at[kind, ex, :, cols],
                send_sem=send.at[kind, h], recv_sem=recv.at[kind, h, ex],
                device_id={"ex": peer}, device_id_type=MESH,
            ).start()
        dst[kind, ex, :, cols] = src[kind, ex, :, cols]

    def z_arrived(kind, h, src, dst, send, recv):
        cols = pl.ds(*spans[h])
        for o in range(1, groups):
            peer = lax.rem(ex + o, groups)
            pltpu.make_async_copy(src.at[kind, peer, :, cols], dst.at[kind, peer, :, cols], recv.at[kind, h, peer]).wait()
        sent = src.at[kind, pl.ds(0, groups - 1), :, cols]
        pltpu.make_async_copy(sent, sent, send.at[kind, h]).wait()

    def fill(kind, h):
        cols = pl.ds(*spans[h])
        if kind == 0:
            value = jnp.dot(either, tokens_ref[:, cols], preferred_element_type=F32)
        else:
            part_cot = cot_ref[:, cols].astype(F32)
            value = sum(jnp.dot(c, (part_cot * g).astype(BF16), preferred_element_type=F32) for c, g in zip(chosen, gates))
        frames[kind, :, :, cols] = value.astype(BF16).reshape(groups, FRAME, spans[h][1])

    fill(0, 0)
    pl.semaphore_wait(barrier, 6 + groups - 1 + 1)
    z_exchange(0, 0, frames, zin, z_send, z_recv)
    fill(0, 1)
    z_exchange(0, 1, frames, zin, z_send, z_recv)
    for h in range(2):
        fill(1, h)
    swaps = [
        pltpu.make_async_remote_copy(
            src_ref=hbm, dst_ref=v.at[1], send_sem=w_send.at[i], recv_sem=w_recv.at[i],
            device_id={"dp": other}, device_id_type=MESH,
        )
        for i, (hbm, v) in enumerate(((wi_hbm, wi), (wo_hbm, wo)))
    ]

    def halves(k, h):
        a, b = (x, y) if h == k else (y, x)
        return (a, b) + spans[h]

    class Gather:
        def __init__(self, k, h):
            self.k, self.h = k, h
            self.a, self.b, self.c0, self.cn = halves(k, h)

        def ref(self, u):
            return xr.at[u, pl.ds(self.k * kind_rows, kind_rows), pl.ds(self.c0, self.cn)]

        def unit(self, db, da):
            return unit_of(self.h ^ self.k, step_of(self.b, db), step_of(self.a, da))

        def send(self, u, db, da, ident):
            ref = self.ref(u)
            pltpu.make_async_remote_copy(
                src_ref=ref, dst_ref=ref, send_sem=ag_send, recv_sem=ag_recv.at[self.k, self.h, ident],
                device_id={"et": self.unit(db, da)}, device_id_type=MESH,
            ).start()

        def wait(self, u, ident):
            ref = self.ref(u)
            pltpu.make_async_copy(ref, ref, ag_recv.at[self.k, self.h, ident]).wait()

        def start(self):
            u = self.unit(0, 0)
            self.send(u, 0, 1, 0)
            self.send(u, 0, -1, 1)
            self.send(u, 0, 2, 2)
            self.send(u, 1, 0, 4)
            self.send(u, -1, 0, 8)

        def near(self):
            u = self.unit(0, -1)
            self.wait(u, 0)
            self.send(u, 1, 0, 5)
            self.send(u, -1, 0, 9)
            u = self.unit(0, 1)
            self.wait(u, 1)
            self.send(u, 1, 0, 6)
            self.send(u, -1, 0, 10)

        def far(self):
            u = self.unit(0, 2)
            self.wait(u, 2)
            self.send(u, 1, 0, 7)
            self.send(u, -1, 0, 11)

        def cross(self, j):
            d = DELTAS[j]
            u = self.unit(-1, d)
            self.wait(u, 4 + j)
            if j < 2:
                self.send(u, 1, 0, 12 + j)
            u = self.unit(1, d)
            self.wait(u, 8 + j)
            if j >= 2:
                self.send(u, -1, 0, 12 + j)

        def last(self):
            for j, d in enumerate(DELTAS):
                self.wait(self.unit(2, d), 12 + j)

    def unpack(kind, h):
        cols = pl.ds(*spans[h])
        z_arrived(kind, h, frames, zin, z_send, z_recv)
        frame_rows = zin[kind, :, :, cols].reshape(groups * FRAME, spans[h][1])
        unit_rows = jnp.dot(pack_ref[...], frame_rows, preferred_element_type=F32)
        xr[et, pl.ds(kind * kind_rows, kind_rows), cols] = unit_rows.astype(BF16)

    g_in = [Gather(0, h) for h in range(2)]
    g_up = [Gather(1, h) for h in range(2)]

    def each(movers, step, *args):
        for m in movers:
            getattr(m, step)(*args)

    half_units = UNITS // 2
    chunks = [
        (1 - doubled, 0, UNITS, 0, single, 0),
        (doubled, 0, half_units, single, 2 * single, UNITS * single),
        (doubled, half_units, half_units, single, 2 * single, 2 * UNITS * single),
    ]
    rows = UNITS * single
    tiles = column_tiles(width, 256)
    full_tiles = width // 256

    def over_tiles(body):
        def step(i, carry):
            body(pl.multiple_of(i * 256, 256), 256)
            return carry

        lax.fori_loop(0, full_tiles, step, 0)
        if width % 256:
            body(full_tiles * 256, width % 256)

    def block(ref, chunk, kind, c0=None, cn=None):
        _, u0, un, r0, rn, _ = chunk
        cols = slice(None) if c0 is None else pl.ds(c0, cn)
        return ref[pl.ds(u0, un), pl.ds(kind * kind_rows + r0, rn), cols].reshape(un * rn, width if c0 is None else cn)

    def put(ref, chunk, kind, c0, cn, value):
        _, u0, un, r0, rn, _ = chunk
        ref[pl.ds(u0, un), pl.ds(kind * kind_rows + r0, rn), pl.ds(c0, cn)] = value.reshape(un, rn, cn)

    def forward_hidden(chunk):
        e, at = chunk[0], chunk[5]
        for q in range(2):
            v = jnp.dot(block(xr, chunk, 0), wi[q, e], preferred_element_type=F32)
            square = v * v
            t = jnp.tanh(gelu_scale * (v + 0.044715 * square * v))
            hid[pl.ds(at, rows), q * hidden:(q + 1) * hidden] = (0.5 * v * (1.0 + t)).astype(BF16)
            dgelu[pl.ds(at, rows), q * hidden:(q + 1) * hidden] = 0.5 * (1.0 + t) + 0.5 * v * (1.0 - t * t) * (
                gelu_scale * (1.0 + 3 * 0.044715 * square)
            )

    def forward_out(chunk):
        e, at = chunk[0], chunk[5]

        def tile(c0, cn):
            total = jnp.dot(hid[pl.ds(at, rows), 0:hidden], wo[0, e, :, pl.ds(c0, cn)], preferred_element_type=F32)
            total += jnp.dot(hid[pl.ds(at, rows), hidden:2 * hidden], wo[1, e, :, pl.ds(c0, cn)], preferred_element_type=F32)
            put(part, chunk, 1, c0, cn, total.astype(BF16))

        over_tiles(tile)

    def backward_slope(chunk):
        e, at = chunk[0], chunk[5]
        for q in range(2):
            back = lax.dot_general(block(xr, chunk, 1), wo[q, e], (((1,), (1,)), ((), ())), preferred_element_type=F32)
            slope_v[pl.ds(at, rows), q * hidden:(q + 1) * hidden] = (
                back * dgelu[pl.ds(at, rows), q * hidden:(q + 1) * hidden]
            ).astype(BF16)

    def backward_input(chunk):
        e, at = chunk[0], chunk[5]

        def tile(c0, cn):
            total = sum(
                lax.dot_general(
                    slope_v[pl.ds(at, rows), q * hidden:(q + 1) * hidden], wi[q, e, pl.ds(c0, cn), :],
                    (((1,), (1,)), ((), ())), preferred_element_type=F32,
                )
                for q in range(2)
            )
            put(part, chunk, 0, c0, cn, total.astype(BF16))

        over_tiles(tile)

    class Scatter:
        def __init__(self, k, h):
            self.k, self.h = k, h
            self.a, self.b, self.c0, self.cn = halves(k, h)

        def ref(self, u):
            return part.at[u, pl.ds(self.k * kind_rows, kind_rows), pl.ds(self.c0, self.cn)]

        def buf(self, slot):
            return rbuf.at[self.k, slot, :, pl.ds(self.c0, self.cn)]

        def unit(self, db, da):
            return unit_of(self.h ^ self.k, step_of(self.b, db), step_of(self.a, da))

        def send(self, u, db, da, slot, ident):
            pltpu.make_async_remote_copy(
                src_ref=self.ref(u), dst_ref=self.buf(slot), send_sem=rs_send,
                recv_sem=rs_recv.at[self.k, self.h, ident],
                device_id={"et": self.unit(db, da)}, device_id_type=MESH,
            ).start()

        def wait(self, slot, ident):
            ref = self.buf(slot)
            pltpu.make_async_copy(ref, ref, rs_recv.at[self.k, self.h, ident]).wait()

        def add(self, u, slots):
            ref = self.ref(u)
            total = ref[...].astype(F32)
            for s in slots:
                total += self.buf(s)[...].astype(F32)
            ref[...] = total.astype(BF16)

        def start(self):
            order = (3, 1, 2, 0)
            for j in order:
                self.send(self.unit(2, DELTAS[j]), 1 if j < 2 else -1, 0, j, j)

        def early(self):
            for j in (3, 1, 2, 0):
                d = DELTAS[j]
                if j < 2:
                    self.send(self.unit(-1, d), -1, 0, 8 + j, 8 + j)
                else:
                    self.send(self.unit(1, d), 1, 0, 4 + j, 4 + j)

        def near(self, j):
            side = 1 if j < 2 else -1
            u = self.unit(side, DELTAS[j])
            self.wait(j, j)
            self.add(u, (j,))
            ident = (4 if j < 2 else 8) + j
            self.send(u, side, 0, ident, ident)

        def cross(self, j):
            u = self.unit(0, DELTAS[j])
            self.wait(4 + j, 4 + j)
            self.wait(8 + j, 8 + j)
            self.add(u, (4 + j, 8 + j))
            if j:
                place = {3: 12, 2: 13, 1: 14}[j]
                self.send(u, 0, DELTAS[j], place, place)

        def last(self):
            total = self.ref(self.unit(0, 0))[...].astype(F32)
            for s in (13, 14, 12):
                self.wait(s, s)
                total += self.buf(s)[...].astype(F32)
            own[pl.ds(self.k * kind_rows, kind_rows), pl.ds(self.c0, self.cn)] = total.astype(BF16)

    s_in = [Scatter(0, h) for h in range(2)]
    s_out = [Scatter(1, h) for h in range(2)]
    first_doubled = doubled == 0

    def tn(lhs, rhs):
        return lax.dot_general(lhs, rhs, (((0,), (0,)), ((), ())), preferred_element_type=F32)

    def whole(kind, role, c0, cn):
        r0, rn = (0, single) if role == 0 else (single, 2 * single)
        return xr[:, pl.ds(kind * kind_rows + r0, rn), pl.ds(c0, cn)].reshape(UNITS * rn, cn)

    def role_rows(ref, role):
        return ref[0:rows, :] if role == 0 else ref[rows:3 * rows, :]

    def gi_tile(c0, cn):
        by_role = [tn(whole(0, role, c0, cn), role_rows(slope_v, role)) for role in range(2)]
        for e in range(2):
            value = jnp.where(first_doubled, by_role[1 - e], by_role[e]).astype(BF16)
            for q in range(2):
                gi_v[q, e, pl.ds(c0, cn), :] = value[:, q * hidden:(q + 1) * hidden]

    def go_tile(c0, cn):
        by_role = [tn(role_rows(hid, role), whole(1, role, c0, cn)) for role in range(2)]
        for e in range(2):
            value = jnp.where(first_doubled, by_role[1 - e], by_role[e]).astype(BF16)
            for q in range(2):
                go_v[q, e, :, pl.ds(c0, cn)] = value[q * hidden:(q + 1) * hidden, :]

    def give(i, v, own_hbm, got_hbm):
        store = pltpu.make_async_copy(v.at[0], own_hbm, g_store.at[i])
        swap = pltpu.make_async_remote_copy(
            src_ref=v.at[1], dst_ref=got_hbm, send_sem=g_send.at[i], recv_sem=g_recv.at[i],
            device_id={"dp": other}, device_id_type=MESH,
        )
        store.start()
        swap.start()
        return store, swap

    def go_back(kind, h):
        cols = pl.ds(*spans[h])
        own_rows = own[pl.ds(kind * kind_rows, kind_rows), cols]
        frames_back[kind, :, :, cols] = tn(pack_ref[...], own_rows).astype(BF16).reshape(groups, FRAME, spans[h][1])
        z_exchange(kind, h, frames_back, zback, zb_send, zb_recv)

    def came_back(kind, h):
        z_arrived(kind, h, frames_back, zback, zb_send, zb_recv)
        return zback[kind, :, :, pl.ds(*spans[h])].reshape(groups * FRAME, spans[h][1])

    def finish_out():
        dots = [0.0, 0.0]
        for h in range(2):
            cols = pl.ds(*spans[h])
            back = came_back(1, h)
            pair = [tn(c, back) for c in chosen]
            layer_ref[:, cols] = (gates[0] * pair[0] + gates[1] * pair[1]).astype(BF16)
            part_cot = cot_ref[:, cols].astype(F32)
            dots = [d + jnp.sum(part_cot * p, axis=1, keepdims=True) for d, p in zip(dots, pair)]
        for k in range(2):
            ggate_ref[k:k + 1, :] = lying(dots[k])

    unpack(0, 0)
    g_in[0].start()
    unpack(0, 1)
    g_in[1].start()
    for h in range(2):
        z_exchange(1, h, frames, zin, z_send, z_recv)
    for c in swaps:
        c.start()
    each(g_in, "near")
    each(g_in, "far")
    each(g_in, "cross", 0)
    each(g_in, "cross", 1)
    for h in range(2):
        unpack(1, h)
        g_up[h].start()
    each(g_in, "cross", 2)
    each(g_in, "cross", 3)
    for c in loads:
        c.wait()
    for c in swaps:
        c.wait()
    each(g_in, "last")
    each(g_up, "near")
    forward_hidden(chunks[0])
    each(g_up, "far")
    forward_hidden(chunks[1])
    forward_hidden(chunks[2])
    each(g_up, "cross", 0)
    forward_out(chunks[0])
    each(g_up, "cross", 1)
    forward_out(chunks[1])
    each(g_up, "cross", 2)
    forward_out(chunks[2])
    each(g_up, "cross", 3)
    each(s_out, "start")
    each(s_out, "early")
    each(g_up, "last")
    backward_slope(chunks[0])
    backward_slope(chunks[1])
    each(s_out, "near", 3)
    each(s_out, "near", 1)
    backward_slope(chunks[2])
    each(s_out, "near", 2)
    each(s_out, "near", 0)
    backward_input(chunks[0])
    backward_input(chunks[1])
    each(s_out, "cross", 3)
    backward_input(chunks[2])
    each(s_in, "start")
    each(s_in, "early")
    each(s_out, "cross", 1)
    each(s_out, "cross", 2)
    each(s_in, "near", 3)
    each(s_in, "near", 1)
    over_tiles(go_tile)
    given = [give(0, go_v, go_own_hbm, go_got_hbm)]
    each(s_out, "cross", 0)
    each(s_in, "near", 2)
    each(s_in, "near", 0)
    for h in range(2):
        s_out[h].last()
        go_back(1, h)
    each(s_in, "cross", 3)
    each(s_in, "cross", 1)
    each(s_in, "cross", 2)
    over_tiles(gi_tile)
    given.append(give(1, gi_v, gi_own_hbm, gi_got_hbm))
    each(s_in, "cross", 0)
    finish_out()
    for h in range(2):
        s_in[h].last()
        go_back(0, h)
    for h in range(2):
        gtok_ref[:, pl.ds(*spans[h])] = tn(either, came_back(0, h)).astype(BF16)

    sent = xr.at[pl.ds(0, UNITS - 1)]
    pltpu.make_async_copy(sent, sent, ag_send).wait()
    sent = part.at[pl.ds(0, UNITS - 1)]
    pltpu.make_async_copy(sent, sent, rs_send).wait()
    for store, swap in given:
        store.wait()
        swap.wait()


def finish_kernel(
    layer_ref, gtok_ref, ggate_ref, gi_own, gi_got, go_own, go_got,
    layer_hbm, gtok_hbm, ggate_hbm, gi_hbm, go_hbm, gi_v, go_v, small_sem, sum_sem,
):
    copies = [
        pltpu.make_async_copy(v, hbm, small_sem.at[i])
        for i, (v, hbm) in enumerate(((layer_ref, layer_hbm), (gtok_ref, gtok_hbm), (ggate_ref, ggate_hbm)))
    ]
    for c in copies:
        c.start()
    for i, (own, got, total, hbm) in enumerate(((gi_own, gi_got, gi_v, gi_hbm), (go_own, go_got, go_v, go_hbm))):
        piece = own.shape[1] // 4
        for e in range(2):
            for n in range(4):
                here = (e, pl.ds(n * piece, piece))
                total[here] = own[here].astype(F32) + got[here].astype(F32)
                copies.append(pltpu.make_async_copy(total.at[here], hbm.at[here], sum_sem.at[i, e, n]))
                copies[-1].start()
    for c in copies:
        c.wait()


def shards(mesh_shape, tokens, gate_probs, expert_ids, copies, weight_in, weight_out, cotangent):
    groups = mesh_shape["ex"]
    count, width = tokens.shape
    hidden = weight_in.shape[2]
    unit_rows = 12 * groups
    kind_rows = 6 * groups
    all_rows = UNITS * kind_rows
    pack = jnp.asarray(pack_matrix(groups), BF16)
    vmem, anywhere = pl.BlockSpec(memory_space=pltpu.VMEM), pl.BlockSpec(memory_space=pl.ANY)
    shape = jax.ShapeDtypeStruct
    dma = pltpu.SemaphoreType.DMA
    results = pl.pallas_call(
        functools.partial(layer_kernel, groups),
        out_shape=(
            shape((count, width), BF16), shape((count, width), BF16), shape((2, count), F32),
            shape(weight_in.shape, BF16), shape(weight_in.shape, BF16),
            shape(weight_out.shape, BF16), shape(weight_out.shape, BF16),
        ),
        in_specs=[pl.BlockSpec(memory_space=pltpu.HBM)] * 8,
        out_specs=(vmem, vmem, vmem, anywhere, anywhere, anywhere, anywhere),
        scratch_shapes=[
            pltpu.VMEM((2, count), jnp.int32), pltpu.SMEM(copies.shape, jnp.int32), pltpu.VMEM(pack.shape, BF16),
            pltpu.VMEM((count, width), BF16), pltpu.VMEM((count, width), BF16), pltpu.VMEM((2, count), F32),
            pltpu.VMEM((2,) + weight_in.shape, BF16),
            pltpu.VMEM((2,) + weight_out.shape, BF16),
            pltpu.VMEM((2, groups, FRAME, width), BF16),
            pltpu.VMEM((2, groups, FRAME, width), BF16),
            pltpu.VMEM((UNITS, unit_rows, width), BF16),
            pltpu.VMEM((UNITS, unit_rows, width), BF16),
            pltpu.VMEM((2, 15, kind_rows, width), BF16),
            pltpu.VMEM((unit_rows, width), BF16),
            pltpu.VMEM((2, groups, FRAME, width), BF16),
            pltpu.VMEM((2, groups, FRAME, width), BF16),
            pltpu.VMEM((all_rows, 2 * hidden), BF16),
            pltpu.VMEM((all_rows, 2 * hidden), BF16),
            pltpu.VMEM((all_rows, 2 * hidden), F32),
            pltpu.VMEM((2,) + weight_in.shape, BF16),
            pltpu.VMEM((2,) + weight_out.shape, BF16),
            dma((6,)), dma((2,)), dma((2,)), dma((2,)),
            dma((2, 2)), dma((2, 2, groups)),
            dma(()), dma((2, 2, 16)),
            dma(()), dma((2, 2, 16)),
            dma((2, 2)), dma((2, 2, groups)),
            dma((2,)), dma((2,)), dma((2,)),
        ],
        compiler_params=pltpu.CompilerParams(
            collective_id=0, has_side_effects=True, vmem_limit_bytes=46 * 2**20
        ),
        name="moe_layer",
    )(*(
        pltpu.with_memory_space_constraint(v, pltpu.HBM)
        for v in (expert_ids.T, copies, pack, tokens, cotangent, gate_probs.T, weight_in, weight_out)
    ))
    hbm = pl.BlockSpec(memory_space=pltpu.HBM)
    layer_out, grad_tokens, grad_gates, grad_in, grad_out = pl.pallas_call(
        finish_kernel,
        out_shape=(
            shape((count, width), BF16), shape((count, width), BF16), shape((2, count), F32),
            shape(weight_in.shape, F32), shape(weight_out.shape, F32),
        ),
        in_specs=[vmem] * 7,
        out_specs=(hbm,) * 5,
        scratch_shapes=[
            pltpu.VMEM(weight_in.shape, F32), pltpu.VMEM(weight_out.shape, F32), dma((3,)), dma((2, 2, 4)),
        ],
        compiler_params=pltpu.CompilerParams(vmem_limit_bytes=8 * 2**20),
        name="replica_sums",
    )(*(pltpu.with_memory_space_constraint(v, pltpu.VMEM) for v in results))
    return layer_out, grad_tokens, grad_gates.T, grad_in, grad_out


def solution(mesh):
    rows = P(("et", "ex", "dp"), None)
    w_in = P("ex", None, ("et", "dp"))
    w_out = P("ex", ("et", "dp"), None)
    return jax.shard_map(
        functools.partial(shards, dict(mesh.shape)),
        mesh=mesh,
        in_specs=(rows, rows, rows, P(), w_in, w_out, rows),
        out_specs=(rows, rows, rows, w_in, w_out),
        check_vma=False,
    )
```

```python
import functools

import jax
import jax.numpy as jnp
import numpy as np
from jax import lax
from jax.experimental import pallas as pl
from jax.experimental.pallas import tpu as pltpu
from jax.sharding import PartitionSpec as P

MESH = pl.DeviceIdType.MESH
SIDE = 4
UNITS = SIDE * SIDE
FRAME = 8
DELTAS = (0, -1, 1, 2)
F32 = jnp.float32
BF16 = jnp.bfloat16
gelu_scale = 0.7978845608028654


def pack_matrix(groups):
    single = 2 * groups
    out = np.zeros((3 * single, groups * FRAME), np.float32)
    for r in range(single):
        out[r, (r // 2) * FRAME + r % 2] = 1
    for r in range(2 * single):
        out[single + r, (r // 4) * FRAME + 2 + r % 4] = 1
    return out


def column_tiles(width, step):
    return [(c, min(step, width - c)) for c in range(0, width, step)]


def layer_kernel(
    groups, ids_hbm, copies_hbm, pack_hbm, tokens_hbm, cot_hbm, gates_hbm, wi_hbm, wo_hbm,
    layer_ref, gtok_ref, ggate_ref, gi_own_hbm, gi_got_hbm, go_own_hbm, go_got_hbm,
    ids_ref, copies_ref, pack_ref, tokens_ref, cot_ref, gates_ref, wi, wo, frames, zin, xr, part, rbuf, own, frames_back, zback, hid, slope_v, dgelu, gi_v, go_v,
    in_load, w_send, w_recv, w_load, z_send, z_recv, ag_send, ag_recv, rs_send, rs_recv, zb_send, zb_recv, g_send, g_recv, g_store,
):
    width = tokens_ref.shape[1]
    hidden = wi.shape[3]
    et = lax.axis_index("et")
    ex = lax.axis_index("ex")
    dp = lax.axis_index("dp")
    y, x = lax.div(et, SIDE), lax.rem(et, SIDE)
    other = 1 - dp
    kind_rows = 6 * groups
    single = 2 * groups
    half_cut = (width // 128 + 1) // 2 * 128

    def step_of(v, d):
        return lax.rem(v + (d + SIDE), SIDE)

    def unit_of(h, b, a):
        return b * SIDE + a if h == 0 else a * SIDE + b

    arrays = [
        pltpu.make_async_copy(hbm, v, in_load.at[i])
        for i, (hbm, v) in enumerate((
            (ids_hbm, ids_ref), (copies_hbm, copies_ref), (gates_hbm, gates_ref),
            (cot_hbm, cot_ref), (tokens_hbm, tokens_ref), (pack_hbm, pack_ref),
        ))
    ]
    for c in arrays:
        c.start()

    zin[...] = jnp.zeros_like(zin)
    zback[...] = jnp.zeros_like(zback)

    barrier = pltpu.get_barrier_semaphore()
    for dev in (
        unit_of(0, y, step_of(x, 1)), unit_of(0, y, step_of(x, -1)),
        unit_of(0, step_of(y, 1), x), unit_of(0, step_of(y, -1), x),
        unit_of(0, y, step_of(x, 2)), unit_of(0, step_of(y, 2), x),
    ):
        pl.semaphore_signal(barrier, inc=1, device_id={"et": dev}, device_id_type=MESH)
    for o in range(1, groups):
        pl.semaphore_signal(barrier, inc=1, device_id={"ex": lax.rem(ex + o, groups)}, device_id_type=MESH)
    pl.semaphore_signal(barrier, inc=1, device_id={"dp": other}, device_id_type=MESH)

    loads = [
        pltpu.make_async_copy(wi_hbm, wi.at[0], w_load.at[0]),
        pltpu.make_async_copy(wo_hbm, wo.at[0], w_load.at[1]),
    ]
    for c in loads:
        c.start()

    for c in arrays:
        c.wait()
    doubled = jnp.where(copies_ref[2 * ex + 1] == 2, 1, 0)
    count = tokens_ref.shape[0]
    square = (count, count)
    down, along = lax.broadcasted_iota(jnp.int32, square, 0), lax.broadcasted_iota(jnp.int32, square, 1)
    diagonal = down == along

    def upright(row):
        return jnp.sum(jnp.where(diagonal, jnp.broadcast_to(row, square), 0.0), axis=1, keepdims=True)

    def lying(column):
        return jnp.sum(jnp.where(diagonal, jnp.broadcast_to(column, square), 0.0), axis=0, keepdims=True)

    ids = [ids_ref[k:k + 1, :] for k in range(2)]
    columns = [upright(v.astype(F32)) for v in ids]
    spots = lax.broadcasted_iota(jnp.int32, (groups * FRAME, count), 0)
    chosen = []
    for k in range(2):
        mine = ids[k].astype(F32)
        same = sum(jnp.where((c == mine) & (down < along), 1.0, 0.0) for c in columns)
        rank = jnp.sum(same, axis=0, keepdims=True).astype(jnp.int32)
        held = jnp.zeros_like(ids[k])
        for e in range(2 * groups):
            held = jnp.where(ids[k] == e, copies_ref[e], held)
        spot = (ids[k] >> 1) * FRAME + jnp.where(held == 2, 2 + rank, rank)
        spot = jnp.where(rank < 2 * held, spot, -1)
        chosen.append(jnp.where(spots == spot, 1.0, 0.0).astype(BF16))
    either = chosen[0] + chosen[1]
    gates = [upright(gates_ref[k:k + 1, :]) for k in range(2)]

    spans = ((0, half_cut), (half_cut, width - half_cut))
    held_rows = pl.ds(0, 6)

    def z_exchange(kind, h, src, dst, send, recv):
        cols = pl.ds(*spans[h])
        for o in range(1, groups):
            peer = lax.rem(ex + o, groups)
            pltpu.make_async_remote_copy(
                src_ref=src.at[kind, peer, held_rows, cols], dst_ref=dst.at[kind, ex, held_rows, cols],
                send_sem=send.at[kind, h], recv_sem=recv.at[kind, h, ex],
                device_id={"ex": peer}, device_id_type=MESH,
            ).start()
        dst[kind, ex, :, cols] = src[kind, ex, :, cols]

    def z_arrived(kind, h, src, dst, send, recv):
        cols = pl.ds(*spans[h])
        for o in range(1, groups):
            peer = lax.rem(ex + o, groups)
            pltpu.make_async_copy(
                src.at[kind, peer, held_rows, cols], dst.at[kind, peer, held_rows, cols], recv.at[kind, h, peer]
            ).wait()
        sent = src.at[kind, pl.ds(0, groups - 1), held_rows, cols]
        pltpu.make_async_copy(sent, sent, send.at[kind, h]).wait()

    def fill(kind, h):
        cols = pl.ds(*spans[h])
        if kind == 0:
            value = jnp.dot(either, tokens_ref[:, cols], preferred_element_type=F32)
        else:
            part_cot = cot_ref[:, cols].astype(F32)
            value = sum(jnp.dot(c, (part_cot * g).astype(BF16), preferred_element_type=F32) for c, g in zip(chosen, gates))
        frames[kind, :, :, cols] = value.astype(BF16).reshape(groups, FRAME, spans[h][1])

    fill(0, 0)
    pl.semaphore_wait(barrier, 6 + groups - 1 + 1)
    z_exchange(0, 0, frames, zin, z_send, z_recv)
    fill(0, 1)
    z_exchange(0, 1, frames, zin, z_send, z_recv)
    for h in range(2):
        fill(1, h)
    swaps = [
        pltpu.make_async_remote_copy(
            src_ref=hbm, dst_ref=v.at[1], send_sem=w_send.at[i], recv_sem=w_recv.at[i],
            device_id={"dp": other}, device_id_type=MESH,
        )
        for i, (hbm, v) in enumerate(((wi_hbm, wi), (wo_hbm, wo)))
    ]

    def halves(k, h):
        a, b = (x, y) if h == k else (y, x)
        return (a, b) + spans[h]

    class Gather:
        def __init__(self, k, h):
            self.k, self.h = k, h
            self.a, self.b, self.c0, self.cn = halves(k, h)

        def ref(self, u):
            return xr.at[u, pl.ds(self.k * kind_rows, kind_rows), pl.ds(self.c0, self.cn)]

        def unit(self, db, da):
            return unit_of(self.h ^ self.k, step_of(self.b, db), step_of(self.a, da))

        def send(self, u, db, da, ident):
            ref = self.ref(u)
            pltpu.make_async_remote_copy(
                src_ref=ref, dst_ref=ref, send_sem=ag_send, recv_sem=ag_recv.at[self.k, self.h, ident],
                device_id={"et": self.unit(db, da)}, device_id_type=MESH,
            ).start()

        def wait(self, u, ident):
            ref = self.ref(u)
            pltpu.make_async_copy(ref, ref, ag_recv.at[self.k, self.h, ident]).wait()

        def start(self):
            u = self.unit(0, 0)
            self.send(u, 0, 1, 0)
            self.send(u, 0, -1, 1)
            self.send(u, 0, 2, 2)
            self.send(u, 1, 0, 4)
            self.send(u, -1, 0, 8)

        def near(self):
            u = self.unit(0, -1)
            self.wait(u, 0)
            self.send(u, 1, 0, 5)
            self.send(u, -1, 0, 9)
            u = self.unit(0, 1)
            self.wait(u, 1)
            self.send(u, 1, 0, 6)
            self.send(u, -1, 0, 10)

        def far(self):
            u = self.unit(0, 2)
            self.wait(u, 2)
            self.send(u, 1, 0, 7)
            self.send(u, -1, 0, 11)

        def cross(self, j):
            d = DELTAS[j]
            u = self.unit(-1, d)
            self.wait(u, 4 + j)
            if j < 2:
                self.send(u, 1, 0, 12 + j)
            u = self.unit(1, d)
            self.wait(u, 8 + j)
            if j >= 2:
                self.send(u, -1, 0, 12 + j)

        def last(self):
            for j, d in enumerate(DELTAS):
                self.wait(self.unit(2, d), 12 + j)

    def unpack(kind, h):
        cols = pl.ds(*spans[h])
        z_arrived(kind, h, frames, zin, z_send, z_recv)
        frame_rows = zin[kind, :, :, cols].reshape(groups * FRAME, spans[h][1])
        unit_rows = jnp.dot(pack_ref[...], frame_rows, preferred_element_type=F32)
        xr[et, pl.ds(kind * kind_rows, kind_rows), cols] = unit_rows.astype(BF16)

    g_in = [Gather(0, h) for h in range(2)]
    g_up = [Gather(1, h) for h in range(2)]

    def each(movers, step, *args):
        for m in movers:
            getattr(m, step)(*args)

    half_units = UNITS // 2
    chunks = [
        (1 - doubled, 0, UNITS, 0, single, 0),
        (doubled, 0, half_units, single, 2 * single, UNITS * single),
        (doubled, half_units, half_units, single, 2 * single, 2 * UNITS * single),
    ]
    rows = UNITS * single
    tiles = column_tiles(width, 256)
    full_tiles = width // 256

    def over_tiles(body):
        def step(i, carry):
            body(pl.multiple_of(i * 256, 256), 256)
            return carry

        lax.fori_loop(0, full_tiles, step, 0)
        if width % 256:
            body(full_tiles * 256, width % 256)

    def block(ref, chunk, kind, c0=None, cn=None):
        _, u0, un, r0, rn, _ = chunk
        cols = slice(None) if c0 is None else pl.ds(c0, cn)
        return ref[pl.ds(u0, un), pl.ds(kind * kind_rows + r0, rn), cols].reshape(un * rn, width if c0 is None else cn)

    def put(ref, chunk, kind, c0, cn, value):
        _, u0, un, r0, rn, _ = chunk
        ref[pl.ds(u0, un), pl.ds(kind * kind_rows + r0, rn), pl.ds(c0, cn)] = value.reshape(un, rn, cn)

    def forward_hidden(chunk):
        e, at = chunk[0], chunk[5]
        for q in range(2):
            v = jnp.dot(block(xr, chunk, 0), wi[q, e], preferred_element_type=F32)
            square = v * v
            t = jnp.tanh(gelu_scale * (v + 0.044715 * square * v))
            hid[pl.ds(at, rows), q * hidden:(q + 1) * hidden] = (0.5 * v * (1.0 + t)).astype(BF16)
            dgelu[pl.ds(at, rows), q * hidden:(q + 1) * hidden] = 0.5 * (1.0 + t) + 0.5 * v * (1.0 - t * t) * (
                gelu_scale * (1.0 + 3 * 0.044715 * square)
            )

    def forward_out(chunk):
        e, at = chunk[0], chunk[5]

        def tile(c0, cn):
            total = jnp.dot(hid[pl.ds(at, rows), 0:hidden], wo[0, e, :, pl.ds(c0, cn)], preferred_element_type=F32)
            total += jnp.dot(hid[pl.ds(at, rows), hidden:2 * hidden], wo[1, e, :, pl.ds(c0, cn)], preferred_element_type=F32)
            put(part, chunk, 1, c0, cn, total.astype(BF16))

        over_tiles(tile)

    def backward_slope(chunk):
        e, at = chunk[0], chunk[5]
        for q in range(2):
            back = lax.dot_general(block(xr, chunk, 1), wo[q, e], (((1,), (1,)), ((), ())), preferred_element_type=F32)
            slope_v[pl.ds(at, rows), q * hidden:(q + 1) * hidden] = (
                back * dgelu[pl.ds(at, rows), q * hidden:(q + 1) * hidden]
            ).astype(BF16)

    def backward_input(chunk):
        e, at = chunk[0], chunk[5]

        def tile(c0, cn):
            total = sum(
                lax.dot_general(
                    slope_v[pl.ds(at, rows), q * hidden:(q + 1) * hidden], wi[q, e, pl.ds(c0, cn), :],
                    (((1,), (1,)), ((), ())), preferred_element_type=F32,
                )
                for q in range(2)
            )
            put(part, chunk, 0, c0, cn, total.astype(BF16))

        over_tiles(tile)

    class Scatter:
        def __init__(self, k, h):
            self.k, self.h = k, h
            self.a, self.b, self.c0, self.cn = halves(k, h)

        def ref(self, u):
            return part.at[u, pl.ds(self.k * kind_rows, kind_rows), pl.ds(self.c0, self.cn)]

        def buf(self, slot):
            return rbuf.at[self.k, slot, :, pl.ds(self.c0, self.cn)]

        def unit(self, db, da):
            return unit_of(self.h ^ self.k, step_of(self.b, db), step_of(self.a, da))

        def send(self, u, db, da, slot, ident):
            pltpu.make_async_remote_copy(
                src_ref=self.ref(u), dst_ref=self.buf(slot), send_sem=rs_send,
                recv_sem=rs_recv.at[self.k, self.h, ident],
                device_id={"et": self.unit(db, da)}, device_id_type=MESH,
            ).start()

        def wait(self, slot, ident):
            ref = self.buf(slot)
            pltpu.make_async_copy(ref, ref, rs_recv.at[self.k, self.h, ident]).wait()

        def add(self, u, slots):
            ref = self.ref(u)
            total = ref[...].astype(F32)
            for s in slots:
                total += self.buf(s)[...].astype(F32)
            ref[...] = total.astype(BF16)

        def start(self):
            order = (3, 1, 2, 0)
            for j in order:
                self.send(self.unit(2, DELTAS[j]), 1 if j < 2 else -1, 0, j, j)

        def early(self):
            for j in (3, 1, 2, 0):
                d = DELTAS[j]
                if j < 2:
                    self.send(self.unit(-1, d), -1, 0, 8 + j, 8 + j)
                else:
                    self.send(self.unit(1, d), 1, 0, 4 + j, 4 + j)

        def near(self, j):
            side = 1 if j < 2 else -1
            u = self.unit(side, DELTAS[j])
            self.wait(j, j)
            self.add(u, (j,))
            ident = (4 if j < 2 else 8) + j
            self.send(u, side, 0, ident, ident)

        def cross(self, j):
            u = self.unit(0, DELTAS[j])
            self.wait(4 + j, 4 + j)
            self.wait(8 + j, 8 + j)
            self.add(u, (4 + j, 8 + j))
            if j:
                place = {3: 12, 2: 13, 1: 14}[j]
                self.send(u, 0, DELTAS[j], place, place)

        def last(self):
            total = self.ref(self.unit(0, 0))[...].astype(F32)
            for s in (13, 14, 12):
                self.wait(s, s)
                total += self.buf(s)[...].astype(F32)
            own[pl.ds(self.k * kind_rows, kind_rows), pl.ds(self.c0, self.cn)] = total.astype(BF16)

    s_in = [Scatter(0, h) for h in range(2)]
    s_out = [Scatter(1, h) for h in range(2)]
    first_doubled = doubled == 0

    def tn(lhs, rhs):
        return lax.dot_general(lhs, rhs, (((0,), (0,)), ((), ())), preferred_element_type=F32)

    def whole(kind, role, c0, cn):
        r0, rn = (0, single) if role == 0 else (single, 2 * single)
        return xr[:, pl.ds(kind * kind_rows + r0, rn), pl.ds(c0, cn)].reshape(UNITS * rn, cn)

    def role_rows(ref, role):
        return ref[0:rows, :] if role == 0 else ref[rows:3 * rows, :]

    def gi_tile(c0, cn):
        by_role = [tn(whole(0, role, c0, cn), role_rows(slope_v, role)) for role in range(2)]
        for e in range(2):
            value = jnp.where(first_doubled, by_role[1 - e], by_role[e]).astype(BF16)
            for q in range(2):
                gi_v[q, e, pl.ds(c0, cn), :] = value[:, q * hidden:(q + 1) * hidden]

    def go_tile(c0, cn):
        by_role = [tn(role_rows(hid, role), whole(1, role, c0, cn)) for role in range(2)]
        for e in range(2):
            value = jnp.where(first_doubled, by_role[1 - e], by_role[e]).astype(BF16)
            for q in range(2):
                go_v[q, e, :, pl.ds(c0, cn)] = value[q * hidden:(q + 1) * hidden, :]

    def give(i, v, own_hbm, got_hbm):
        store = pltpu.make_async_copy(v.at[0], own_hbm, g_store.at[i])
        swap = pltpu.make_async_remote_copy(
            src_ref=v.at[1], dst_ref=got_hbm, send_sem=g_send.at[i], recv_sem=g_recv.at[i],
            device_id={"dp": other}, device_id_type=MESH,
        )
        store.start()
        swap.start()
        return store, swap

    def go_back(kind, h):
        cols = pl.ds(*spans[h])
        own_rows = own[pl.ds(kind * kind_rows, kind_rows), cols]
        frames_back[kind, :, :, cols] = tn(pack_ref[...], own_rows).astype(BF16).reshape(groups, FRAME, spans[h][1])
        z_exchange(kind, h, frames_back, zback, zb_send, zb_recv)

    def came_back(kind, h):
        z_arrived(kind, h, frames_back, zback, zb_send, zb_recv)
        return zback[kind, :, :, pl.ds(*spans[h])].reshape(groups * FRAME, spans[h][1])

    def finish_out():
        dots = [0.0, 0.0]
        for h in range(2):
            cols = pl.ds(*spans[h])
            back = came_back(1, h)
            pair = [tn(c, back) for c in chosen]
            layer_ref[:, cols] = (gates[0] * pair[0] + gates[1] * pair[1]).astype(BF16)
            part_cot = cot_ref[:, cols].astype(F32)
            dots = [d + jnp.sum(part_cot * p, axis=1, keepdims=True) for d, p in zip(dots, pair)]
        for k in range(2):
            ggate_ref[k:k + 1, :] = lying(dots[k])

    unpack(0, 0)
    g_in[0].start()
    unpack(0, 1)
    g_in[1].start()
    for h in range(2):
        z_exchange(1, h, frames, zin, z_send, z_recv)
    for c in swaps:
        c.start()
    each(g_in, "near")
    each(g_in, "far")
    each(g_in, "cross", 0)
    each(g_in, "cross", 1)
    for h in range(2):
        unpack(1, h)
        g_up[h].start()
    each(g_in, "cross", 2)
    each(g_in, "cross", 3)
    for c in loads:
        c.wait()
    for c in swaps:
        c.wait()
    each(g_in, "last")
    each(g_up, "near")
    forward_hidden(chunks[0])
    each(g_up, "far")
    forward_hidden(chunks[1])
    forward_hidden(chunks[2])
    each(g_up, "cross", 0)
    forward_out(chunks[0])
    each(g_up, "cross", 1)
    forward_out(chunks[1])
    each(g_up, "cross", 2)
    forward_out(chunks[2])
    each(g_up, "cross", 3)
    each(s_out, "start")
    each(s_out, "early")
    each(g_up, "last")
    backward_slope(chunks[0])
    backward_slope(chunks[1])
    each(s_out, "near", 3)
    each(s_out, "near", 1)
    backward_slope(chunks[2])
    each(s_out, "near", 2)
    each(s_out, "near", 0)
    backward_input(chunks[0])
    backward_input(chunks[1])
    each(s_out, "cross", 3)
    backward_input(chunks[2])
    each(s_in, "start")
    each(s_in, "early")
    each(s_out, "cross", 1)
    each(s_out, "cross", 2)
    each(s_in, "near", 3)
    each(s_in, "near", 1)
    over_tiles(go_tile)
    given = [give(0, go_v, go_own_hbm, go_got_hbm)]
    each(s_out, "cross", 0)
    each(s_in, "near", 2)
    each(s_in, "near", 0)
    for h in range(2):
        s_out[h].last()
        go_back(1, h)
    each(s_in, "cross", 3)
    each(s_in, "cross", 1)
    each(s_in, "cross", 2)
    over_tiles(gi_tile)
    given.append(give(1, gi_v, gi_own_hbm, gi_got_hbm))
    each(s_in, "cross", 0)
    for h in range(2):
        s_in[h].last()
        go_back(0, h)
    finish_out()
    for h in range(2):
        gtok_ref[:, pl.ds(*spans[h])] = tn(either, came_back(0, h)).astype(BF16)

    sent = xr.at[pl.ds(0, UNITS - 1)]
    pltpu.make_async_copy(sent, sent, ag_send).wait()
    sent = part.at[pl.ds(0, UNITS - 1)]
    pltpu.make_async_copy(sent, sent, rs_send).wait()
    for store, swap in given:
        store.wait()
        swap.wait()


def finish_kernel(
    layer_ref, gtok_ref, ggate_ref, gi_own, gi_got, go_own, go_got,
    layer_hbm, gtok_hbm, ggate_hbm, gi_hbm, go_hbm, gi_v, go_v, small_sem, sum_sem,
):
    copies = [
        pltpu.make_async_copy(v, hbm, small_sem.at[i])
        for i, (v, hbm) in enumerate(((layer_ref, layer_hbm), (gtok_ref, gtok_hbm), (ggate_ref, ggate_hbm)))
    ]
    for c in copies:
        c.start()
    for i, (own, got, total, hbm) in enumerate(((gi_own, gi_got, gi_v, gi_hbm), (go_own, go_got, go_v, go_hbm))):
        piece = own.shape[1] // 4
        for e in range(2):
            for n in range(4):
                here = (e, pl.ds(n * piece, piece))
                total[here] = own[here].astype(F32) + got[here].astype(F32)
                copies.append(pltpu.make_async_copy(total.at[here], hbm.at[here], sum_sem.at[i, e, n]))
                copies[-1].start()
    for c in copies:
        c.wait()


def shards(mesh_shape, tokens, gate_probs, expert_ids, copies, weight_in, weight_out, cotangent):
    groups = mesh_shape["ex"]
    count, width = tokens.shape
    hidden = weight_in.shape[2]
    unit_rows = 12 * groups
    kind_rows = 6 * groups
    all_rows = UNITS * kind_rows
    pack = jnp.asarray(pack_matrix(groups), BF16)
    vmem, anywhere = pl.BlockSpec(memory_space=pltpu.VMEM), pl.BlockSpec(memory_space=pl.ANY)
    shape = jax.ShapeDtypeStruct
    dma = pltpu.SemaphoreType.DMA
    results = pl.pallas_call(
        functools.partial(layer_kernel, groups),
        out_shape=(
            shape((count, width), BF16), shape((count, width), BF16), shape((2, count), F32),
            shape(weight_in.shape, BF16), shape(weight_in.shape, BF16),
            shape(weight_out.shape, BF16), shape(weight_out.shape, BF16),
        ),
        in_specs=[pl.BlockSpec(memory_space=pltpu.HBM)] * 8,
        out_specs=(vmem, vmem, vmem, anywhere, anywhere, anywhere, anywhere),
        scratch_shapes=[
            pltpu.VMEM((2, count), jnp.int32), pltpu.SMEM(copies.shape, jnp.int32), pltpu.VMEM(pack.shape, BF16),
            pltpu.VMEM((count, width), BF16), pltpu.VMEM((count, width), BF16), pltpu.VMEM((2, count), F32),
            pltpu.VMEM((2,) + weight_in.shape, BF16),
            pltpu.VMEM((2,) + weight_out.shape, BF16),
            pltpu.VMEM((2, groups, FRAME, width), BF16),
            pltpu.VMEM((2, groups, FRAME, width), BF16),
            pltpu.VMEM((UNITS, unit_rows, width), BF16),
            pltpu.VMEM((UNITS, unit_rows, width), BF16),
            pltpu.VMEM((2, 15, kind_rows, width), BF16),
            pltpu.VMEM((unit_rows, width), BF16),
            pltpu.VMEM((2, groups, FRAME, width), BF16),
            pltpu.VMEM((2, groups, FRAME, width), BF16),
            pltpu.VMEM((all_rows, 2 * hidden), BF16),
            pltpu.VMEM((all_rows, 2 * hidden), BF16),
            pltpu.VMEM((all_rows, 2 * hidden), F32),
            pltpu.VMEM((2,) + weight_in.shape, BF16),
            pltpu.VMEM((2,) + weight_out.shape, BF16),
            dma((6,)), dma((2,)), dma((2,)), dma((2,)),
            dma((2, 2)), dma((2, 2, groups)),
            dma(()), dma((2, 2, 16)),
            dma(()), dma((2, 2, 16)),
            dma((2, 2)), dma((2, 2, groups)),
            dma((2,)), dma((2,)), dma((2,)),
        ],
        compiler_params=pltpu.CompilerParams(
            collective_id=0, has_side_effects=True, vmem_limit_bytes=46 * 2**20
        ),
        name="moe_layer",
    )(*(
        pltpu.with_memory_space_constraint(v, pltpu.HBM)
        for v in (expert_ids.T, copies, pack, tokens, cotangent, gate_probs.T, weight_in, weight_out)
    ))
    hbm = pl.BlockSpec(memory_space=pltpu.HBM)
    layer_out, grad_tokens, grad_gates, grad_in, grad_out = pl.pallas_call(
        finish_kernel,
        out_shape=(
            shape((count, width), BF16), shape((count, width), BF16), shape((2, count), F32),
            shape(weight_in.shape, F32), shape(weight_out.shape, F32),
        ),
        in_specs=[vmem] * 7,
        out_specs=(hbm,) * 5,
        scratch_shapes=[
            pltpu.VMEM(weight_in.shape, F32), pltpu.VMEM(weight_out.shape, F32), dma((3,)), dma((2, 2, 4)),
        ],
        compiler_params=pltpu.CompilerParams(vmem_limit_bytes=8 * 2**20),
        name="replica_sums",
    )(*(pltpu.with_memory_space_constraint(v, pltpu.VMEM) for v in results))
    return layer_out, grad_tokens, grad_gates.T, grad_in, grad_out


def solution(mesh):
    rows = P(("et", "ex", "dp"), None)
    w_in = P("ex", None, ("et", "dp"))
    w_out = P("ex", ("et", "dp"), None)
    return jax.shard_map(
        functools.partial(shards, dict(mesh.shape)),
        mesh=mesh,
        in_specs=(rows, rows, rows, P(), w_in, w_out, rows),
        out_specs=(rows, rows, rows, w_in, w_out),
        check_vma=False,
    )
```

```python
import functools

import jax
import jax.numpy as jnp
import numpy as np
from jax import lax
from jax.experimental import pallas as pl
from jax.experimental.pallas import tpu as pltpu
from jax.sharding import PartitionSpec as P

MESH = pl.DeviceIdType.MESH
SIDE = 4
UNITS = SIDE * SIDE
FRAME = 8
DELTAS = (0, -1, 1, 2)
F32 = jnp.float32
BF16 = jnp.bfloat16
gelu_scale = 0.7978845608028654


def pack_matrix(groups):
    single = 2 * groups
    out = np.zeros((3 * single, groups * FRAME), np.float32)
    for r in range(single):
        out[r, (r // 2) * FRAME + r % 2] = 1
    for r in range(2 * single):
        out[single + r, (r // 4) * FRAME + 2 + r % 4] = 1
    return out


def column_tiles(width, step):
    return [(c, min(step, width - c)) for c in range(0, width, step)]


def layer_kernel(
    groups, ids_hbm, copies_hbm, pack_hbm, tokens_hbm, cot_hbm, gates_hbm, wi_hbm, wo_hbm,
    layer_ref, gtok_ref, ggate_ref, gi_own_hbm, gi_got_hbm, go_own_hbm, go_got_hbm,
    ids_ref, copies_ref, pack_ref, tokens_ref, cot_ref, gates_ref, wi, wo, frames, zin, xr, part, rbuf, own, frames_back, zback, hid, slope_v, dgelu, gi_v, go_v,
    in_load, w_send, w_recv, w_load, z_send, z_recv, ag_send, ag_recv, rs_send, rs_recv, zb_send, zb_recv, g_send, g_recv, g_store,
):
    width = tokens_ref.shape[1]
    hidden = wi.shape[3]
    et = lax.axis_index("et")
    ex = lax.axis_index("ex")
    dp = lax.axis_index("dp")
    y, x = lax.div(et, SIDE), lax.rem(et, SIDE)
    other = 1 - dp
    kind_rows = 6 * groups
    single = 2 * groups
    half_cut = (width // 128 + 1) // 2 * 128

    def step_of(v, d):
        return lax.rem(v + (d + SIDE), SIDE)

    def unit_of(h, b, a):
        return b * SIDE + a if h == 0 else a * SIDE + b

    arrays = [
        pltpu.make_async_copy(hbm, v, in_load.at[i])
        for i, (hbm, v) in enumerate((
            (ids_hbm, ids_ref), (copies_hbm, copies_ref), (gates_hbm, gates_ref),
            (cot_hbm, cot_ref), (tokens_hbm, tokens_ref), (pack_hbm, pack_ref),
        ))
    ]
    for c in arrays:
        c.start()

    zin[...] = jnp.zeros_like(zin)
    zback[...] = jnp.zeros_like(zback)

    barrier = pltpu.get_barrier_semaphore()
    for dev in (
        unit_of(0, y, step_of(x, 1)), unit_of(0, y, step_of(x, -1)),
        unit_of(0, step_of(y, 1), x), unit_of(0, step_of(y, -1), x),
        unit_of(0, y, step_of(x, 2)), unit_of(0, step_of(y, 2), x),
    ):
        pl.semaphore_signal(barrier, inc=1, device_id={"et": dev}, device_id_type=MESH)
    for o in range(1, groups):
        pl.semaphore_signal(barrier, inc=1, device_id={"ex": lax.rem(ex + o, groups)}, device_id_type=MESH)
    pl.semaphore_signal(barrier, inc=1, device_id={"dp": other}, device_id_type=MESH)

    loads = [
        pltpu.make_async_copy(wi_hbm, wi.at[0], w_load.at[0]),
        pltpu.make_async_copy(wo_hbm, wo.at[0], w_load.at[1]),
    ]
    for c in loads:
        c.start()

    for c in arrays:
        c.wait()
    doubled = jnp.where(copies_ref[2 * ex + 1] == 2, 1, 0)
    count = tokens_ref.shape[0]
    square = (count, count)
    down, along = lax.broadcasted_iota(jnp.int32, square, 0), lax.broadcasted_iota(jnp.int32, square, 1)
    diagonal = down == along

    def upright(row):
        return jnp.sum(jnp.where(diagonal, jnp.broadcast_to(row, square), 0.0), axis=1, keepdims=True)

    def lying(column):
        return jnp.sum(jnp.where(diagonal, jnp.broadcast_to(column, square), 0.0), axis=0, keepdims=True)

    ids = [ids_ref[k:k + 1, :] for k in range(2)]
    columns = [upright(v.astype(F32)) for v in ids]
    spots = lax.broadcasted_iota(jnp.int32, (groups * FRAME, count), 0)
    chosen = []
    for k in range(2):
        mine = ids[k].astype(F32)
        same = sum(jnp.where((c == mine) & (down < along), 1.0, 0.0) for c in columns)
        rank = jnp.sum(same, axis=0, keepdims=True).astype(jnp.int32)
        held = jnp.zeros_like(ids[k])
        for e in range(2 * groups):
            held = jnp.where(ids[k] == e, copies_ref[e], held)
        spot = (ids[k] >> 1) * FRAME + jnp.where(held == 2, 2 + rank, rank)
        spot = jnp.where(rank < 2 * held, spot, -1)
        chosen.append(jnp.where(spots == spot, 1.0, 0.0).astype(BF16))
    either = chosen[0] + chosen[1]
    gates = [upright(gates_ref[k:k + 1, :]) for k in range(2)]

    spans = ((0, half_cut), (half_cut, width - half_cut))
    held_rows = pl.ds(0, 6)

    def z_exchange(kind, h, src, dst, send, recv):
        cols = pl.ds(*spans[h])
        for o in range(1, groups):
            peer = lax.rem(ex + o, groups)
            pltpu.make_async_remote_copy(
                src_ref=src.at[kind, peer, held_rows, cols], dst_ref=dst.at[kind, ex, held_rows, cols],
                send_sem=send.at[kind, h], recv_sem=recv.at[kind, h, ex],
                device_id={"ex": peer}, device_id_type=MESH,
            ).start()
        dst[kind, ex, :, cols] = src[kind, ex, :, cols]

    def z_arrived(kind, h, src, dst, send, recv):
        cols = pl.ds(*spans[h])
        for o in range(1, groups):
            peer = lax.rem(ex + o, groups)
            pltpu.make_async_copy(
                src.at[kind, peer, held_rows, cols], dst.at[kind, peer, held_rows, cols], recv.at[kind, h, peer]
            ).wait()
        sent = src.at[kind, pl.ds(0, groups - 1), held_rows, cols]
        pltpu.make_async_copy(sent, sent, send.at[kind, h]).wait()

    def fill(kind, h):
        cols = pl.ds(*spans[h])
        if kind == 0:
            value = jnp.dot(either, tokens_ref[:, cols], preferred_element_type=F32)
        else:
            part_cot = cot_ref[:, cols].astype(F32)
            value = sum(jnp.dot(c, (part_cot * g).astype(BF16), preferred_element_type=F32) for c, g in zip(chosen, gates))
        frames[kind, :, :, cols] = value.astype(BF16).reshape(groups, FRAME, spans[h][1])

    fill(0, 0)
    pl.semaphore_wait(barrier, 6 + groups - 1 + 1)
    z_exchange(0, 0, frames, zin, z_send, z_recv)
    fill(0, 1)
    z_exchange(0, 1, frames, zin, z_send, z_recv)
    for h in range(2):
        fill(1, h)
    swaps = [
        pltpu.make_async_remote_copy(
            src_ref=hbm, dst_ref=v.at[1], send_sem=w_send.at[i], recv_sem=w_recv.at[i],
            device_id={"dp": other}, device_id_type=MESH,
        )
        for i, (hbm, v) in enumerate(((wi_hbm, wi), (wo_hbm, wo)))
    ]

    def halves(k, h):
        a, b = (x, y) if h == k else (y, x)
        return (a, b) + spans[h]

    class Gather:
        def __init__(self, k, h):
            self.k, self.h = k, h
            self.a, self.b, self.c0, self.cn = halves(k, h)

        def ref(self, u):
            return xr.at[u, pl.ds(self.k * kind_rows, kind_rows), pl.ds(self.c0, self.cn)]

        def unit(self, db, da):
            return unit_of(self.h ^ self.k, step_of(self.b, db), step_of(self.a, da))

        def send(self, u, db, da, ident):
            ref = self.ref(u)
            pltpu.make_async_remote_copy(
                src_ref=ref, dst_ref=ref, send_sem=ag_send, recv_sem=ag_recv.at[self.k, self.h, ident],
                device_id={"et": self.unit(db, da)}, device_id_type=MESH,
            ).start()

        def wait(self, u, ident):
            ref = self.ref(u)
            pltpu.make_async_copy(ref, ref, ag_recv.at[self.k, self.h, ident]).wait()

        def start(self):
            u = self.unit(0, 0)
            self.send(u, 0, 1, 0)
            self.send(u, 0, -1, 1)
            self.send(u, 0, 2, 2)
            self.send(u, 1, 0, 4)
            self.send(u, -1, 0, 8)

        def near(self):
            u = self.unit(0, -1)
            self.wait(u, 0)
            self.send(u, 1, 0, 5)
            self.send(u, -1, 0, 9)
            u = self.unit(0, 1)
            self.wait(u, 1)
            self.send(u, 1, 0, 6)
            self.send(u, -1, 0, 10)

        def far(self):
            u = self.unit(0, 2)
            self.wait(u, 2)
            self.send(u, 1, 0, 7)
            self.send(u, -1, 0, 11)

        def cross(self, j):
            d = DELTAS[j]
            u = self.unit(-1, d)
            self.wait(u, 4 + j)
            if j < 2:
                self.send(u, 1, 0, 12 + j)
            u = self.unit(1, d)
            self.wait(u, 8 + j)
            if j >= 2:
                self.send(u, -1, 0, 12 + j)

        def last(self):
            for j, d in enumerate(DELTAS):
                self.wait(self.unit(2, d), 12 + j)

    def unpack(kind, h):
        cols = pl.ds(*spans[h])
        z_arrived(kind, h, frames, zin, z_send, z_recv)
        frame_rows = zin[kind, :, :, cols].reshape(groups * FRAME, spans[h][1])
        unit_rows = jnp.dot(pack_ref[...], frame_rows, preferred_element_type=F32)
        xr[et, pl.ds(kind * kind_rows, kind_rows), cols] = unit_rows.astype(BF16)

    g_in = [Gather(0, h) for h in range(2)]
    g_up = [Gather(1, h) for h in range(2)]

    def each(movers, step, *args):
        for m in movers:
            getattr(m, step)(*args)

    half_units = UNITS // 2
    chunks = [
        (1 - doubled, 0, UNITS, 0, single, 0),
        (doubled, 0, half_units, single, 2 * single, UNITS * single),
        (doubled, half_units, half_units, single, 2 * single, 2 * UNITS * single),
    ]
    rows = UNITS * single
    tiles = column_tiles(width, 256)
    full_tiles = width // 256

    def over_tiles(body):
        def step(i, carry):
            body(pl.multiple_of(i * 256, 256), 256)
            return carry

        lax.fori_loop(0, full_tiles, step, 0)
        if width % 256:
            body(full_tiles * 256, width % 256)

    def block(ref, chunk, kind, c0=None, cn=None):
        _, u0, un, r0, rn, _ = chunk
        cols = slice(None) if c0 is None else pl.ds(c0, cn)
        return ref[pl.ds(u0, un), pl.ds(kind * kind_rows + r0, rn), cols].reshape(un * rn, width if c0 is None else cn)

    def put(ref, chunk, kind, c0, cn, value):
        _, u0, un, r0, rn, _ = chunk
        ref[pl.ds(u0, un), pl.ds(kind * kind_rows + r0, rn), pl.ds(c0, cn)] = value.reshape(un, rn, cn)

    def forward_hidden(chunk):
        e, at = chunk[0], chunk[5]
        for q in range(2):
            v = jnp.dot(block(xr, chunk, 0), wi[q, e], preferred_element_type=F32)
            square = v * v
            t = jnp.tanh(gelu_scale * (v + 0.044715 * square * v))
            hid[pl.ds(at, rows), q * hidden:(q + 1) * hidden] = (0.5 * v * (1.0 + t)).astype(BF16)
            dgelu[pl.ds(at, rows), q * hidden:(q + 1) * hidden] = 0.5 * (1.0 + t) + 0.5 * v * (1.0 - t * t) * (
                gelu_scale * (1.0 + 3 * 0.044715 * square)
            )

    def forward_out(chunk):
        e, at = chunk[0], chunk[5]

        def tile(c0, cn):
            total = jnp.dot(hid[pl.ds(at, rows), 0:hidden], wo[0, e, :, pl.ds(c0, cn)], preferred_element_type=F32)
            total += jnp.dot(hid[pl.ds(at, rows), hidden:2 * hidden], wo[1, e, :, pl.ds(c0, cn)], preferred_element_type=F32)
            put(part, chunk, 1, c0, cn, total.astype(BF16))

        over_tiles(tile)

    def backward_slope(chunk):
        e, at = chunk[0], chunk[5]
        for q in range(2):
            back = lax.dot_general(block(xr, chunk, 1), wo[q, e], (((1,), (1,)), ((), ())), preferred_element_type=F32)
            slope_v[pl.ds(at, rows), q * hidden:(q + 1) * hidden] = (
                back * dgelu[pl.ds(at, rows), q * hidden:(q + 1) * hidden]
            ).astype(BF16)

    def backward_input(chunk):
        e, at = chunk[0], chunk[5]

        def tile(c0, cn):
            total = sum(
                lax.dot_general(
                    slope_v[pl.ds(at, rows), q * hidden:(q + 1) * hidden], wi[q, e, pl.ds(c0, cn), :],
                    (((1,), (1,)), ((), ())), preferred_element_type=F32,
                )
                for q in range(2)
            )
            put(part, chunk, 0, c0, cn, total.astype(BF16))

        over_tiles(tile)

    class Scatter:
        def __init__(self, k, h):
            self.k, self.h = k, h
            self.a, self.b, self.c0, self.cn = halves(k, h)

        def ref(self, u):
            return part.at[u, pl.ds(self.k * kind_rows, kind_rows), pl.ds(self.c0, self.cn)]

        def buf(self, slot):
            return rbuf.at[self.k, slot, :, pl.ds(self.c0, self.cn)]

        def unit(self, db, da):
            return unit_of(self.h ^ self.k, step_of(self.b, db), step_of(self.a, da))

        def send(self, u, db, da, slot, ident):
            pltpu.make_async_remote_copy(
                src_ref=self.ref(u), dst_ref=self.buf(slot), send_sem=rs_send,
                recv_sem=rs_recv.at[self.k, self.h, ident],
                device_id={"et": self.unit(db, da)}, device_id_type=MESH,
            ).start()

        def wait(self, slot, ident):
            ref = self.buf(slot)
            pltpu.make_async_copy(ref, ref, rs_recv.at[self.k, self.h, ident]).wait()

        def add(self, u, slots):
            ref = self.ref(u)
            total = ref[...].astype(F32)
            for s in slots:
                total += self.buf(s)[...].astype(F32)
            ref[...] = total.astype(BF16)

        def start(self):
            order = (3, 1, 2, 0)
            for j in order:
                self.send(self.unit(2, DELTAS[j]), 1 if j < 2 else -1, 0, j, j)

        def early(self):
            for j in (3, 1, 2, 0):
                d = DELTAS[j]
                if j < 2:
                    self.send(self.unit(-1, d), -1, 0, 8 + j, 8 + j)
                else:
                    self.send(self.unit(1, d), 1, 0, 4 + j, 4 + j)

        def near(self, j):
            side = 1 if j < 2 else -1
            u = self.unit(side, DELTAS[j])
            self.wait(j, j)
            self.add(u, (j,))
            ident = (4 if j < 2 else 8) + j
            self.send(u, side, 0, ident, ident)

        def cross(self, j):
            u = self.unit(0, DELTAS[j])
            self.wait(4 + j, 4 + j)
            self.wait(8 + j, 8 + j)
            self.add(u, (4 + j, 8 + j))
            if j:
                place = {3: 12, 2: 13, 1: 14}[j]
                self.send(u, 0, DELTAS[j], place, place)

        def last(self):
            total = self.ref(self.unit(0, 0))[...].astype(F32)
            for s in (13, 14, 12):
                self.wait(s, s)
                total += self.buf(s)[...].astype(F32)
            own[pl.ds(self.k * kind_rows, kind_rows), pl.ds(self.c0, self.cn)] = total.astype(BF16)

    s_in = [Scatter(0, h) for h in range(2)]
    s_out = [Scatter(1, h) for h in range(2)]
    first_doubled = doubled == 0

    def tn(lhs, rhs):
        return lax.dot_general(lhs, rhs, (((0,), (0,)), ((), ())), preferred_element_type=F32)

    def whole(kind, role, c0, cn):
        r0, rn = (0, single) if role == 0 else (single, 2 * single)
        return xr[:, pl.ds(kind * kind_rows + r0, rn), pl.ds(c0, cn)].reshape(UNITS * rn, cn)

    def role_rows(ref, role):
        return ref[0:rows, :] if role == 0 else ref[rows:3 * rows, :]

    def gi_tile(c0, cn):
        by_role = [tn(whole(0, role, c0, cn), role_rows(slope_v, role)) for role in range(2)]
        for e in range(2):
            value = jnp.where(first_doubled, by_role[1 - e], by_role[e]).astype(BF16)
            for q in range(2):
                gi_v[q, e, pl.ds(c0, cn), :] = value[:, q * hidden:(q + 1) * hidden]

    def go_tile(c0, cn):
        by_role = [tn(role_rows(hid, role), whole(1, role, c0, cn)) for role in range(2)]
        for e in range(2):
            value = jnp.where(first_doubled, by_role[1 - e], by_role[e]).astype(BF16)
            for q in range(2):
                go_v[q, e, :, pl.ds(c0, cn)] = value[q * hidden:(q + 1) * hidden, :]

    def give(i, v, own_hbm, got_hbm):
        store = pltpu.make_async_copy(v.at[0], own_hbm, g_store.at[i])
        swap = pltpu.make_async_remote_copy(
            src_ref=v.at[1], dst_ref=got_hbm, send_sem=g_send.at[i], recv_sem=g_recv.at[i],
            device_id={"dp": other}, device_id_type=MESH,
        )
        store.start()
        swap.start()
        return store, swap

    def go_back(kind, h):
        cols = pl.ds(*spans[h])
        own_rows = own[pl.ds(kind * kind_rows, kind_rows), cols]
        frames_back[kind, :, :, cols] = tn(pack_ref[...], own_rows).astype(BF16).reshape(groups, FRAME, spans[h][1])
        z_exchange(kind, h, frames_back, zback, zb_send, zb_recv)

    def came_back(kind, h):
        z_arrived(kind, h, frames_back, zback, zb_send, zb_recv)
        return zback[kind, :, :, pl.ds(*spans[h])].reshape(groups * FRAME, spans[h][1])

    def finish_out():
        dots = [0.0, 0.0]
        for h in range(2):
            cols = pl.ds(*spans[h])
            back = came_back(1, h)
            pair = [tn(c, back) for c in chosen]
            layer_ref[:, cols] = (gates[0] * pair[0] + gates[1] * pair[1]).astype(BF16)
            part_cot = cot_ref[:, cols].astype(F32)
            dots = [d + jnp.sum(part_cot * p, axis=1, keepdims=True) for d, p in zip(dots, pair)]
        for k in range(2):
            ggate_ref[k:k + 1, :] = lying(dots[k])

    unpack(0, 0)
    g_in[0].start()
    z_exchange(1, 0, frames, zin, z_send, z_recv)
    unpack(0, 1)
    g_in[1].start()
    z_exchange(1, 1, frames, zin, z_send, z_recv)
    for c in swaps:
        c.start()
    each(g_in, "near")
    each(g_in, "far")
    each(g_in, "cross", 0)
    each(g_in, "cross", 1)
    for h in range(2):
        unpack(1, h)
        g_up[h].start()
    each(g_in, "cross", 2)
    each(g_in, "cross", 3)
    for c in loads:
        c.wait()
    for c in swaps:
        c.wait()
    each(g_in, "last")
    each(g_up, "near")
    forward_hidden(chunks[0])
    each(g_up, "far")
    forward_hidden(chunks[1])
    forward_hidden(chunks[2])
    each(g_up, "cross", 0)
    forward_out(chunks[0])
    each(g_up, "cross", 1)
    forward_out(chunks[1])
    each(g_up, "cross", 2)
    forward_out(chunks[2])
    each(s_out, "start")
    each(s_out, "early")
    each(g_up, "cross", 3)
    each(g_up, "last")
    backward_slope(chunks[0])
    backward_slope(chunks[1])
    each(s_out, "near", 3)
    each(s_out, "near", 1)
    backward_slope(chunks[2])
    each(s_out, "near", 2)
    each(s_out, "near", 0)
    backward_input(chunks[0])
    backward_input(chunks[1])
    each(s_out, "cross", 3)
    backward_input(chunks[2])
    each(s_in, "start")
    each(s_in, "early")
    each(s_out, "cross", 1)
    each(s_out, "cross", 2)
    each(s_in, "near", 3)
    each(s_in, "near", 1)
    over_tiles(go_tile)
    given = [give(0, go_v, go_own_hbm, go_got_hbm)]
    each(s_out, "cross", 0)
    each(s_in, "near", 2)
    each(s_in, "near", 0)
    each(s_in, "cross", 3)
    each(s_in, "cross", 1)
    each(s_in, "cross", 2)
    for h in range(2):
        s_out[h].last()
        go_back(1, h)
    over_tiles(gi_tile)
    given.append(give(1, gi_v, gi_own_hbm, gi_got_hbm))
    each(s_in, "cross", 0)
    for h in range(2):
        s_in[h].last()
        go_back(0, h)
    finish_out()
    for h in range(2):
        gtok_ref[:, pl.ds(*spans[h])] = tn(either, came_back(0, h)).astype(BF16)

    sent = xr.at[pl.ds(0, UNITS - 1)]
    pltpu.make_async_copy(sent, sent, ag_send).wait()
    sent = part.at[pl.ds(0, UNITS - 1)]
    pltpu.make_async_copy(sent, sent, rs_send).wait()
    for store, swap in given:
        store.wait()
        swap.wait()


def finish_kernel(
    layer_ref, gtok_ref, ggate_ref, gi_own, gi_got, go_own, go_got,
    layer_hbm, gtok_hbm, ggate_hbm, gi_hbm, go_hbm, gi_v, go_v, small_sem, sum_sem,
):
    copies = [
        pltpu.make_async_copy(v, hbm, small_sem.at[i])
        for i, (v, hbm) in enumerate(((layer_ref, layer_hbm), (gtok_ref, gtok_hbm), (ggate_ref, ggate_hbm)))
    ]
    for c in copies:
        c.start()
    for i, (own, got, total, hbm) in enumerate(((gi_own, gi_got, gi_v, gi_hbm), (go_own, go_got, go_v, go_hbm))):
        piece = own.shape[1] // 4
        for e in range(2):
            for n in range(4):
                here = (e, pl.ds(n * piece, piece))
                total[here] = own[here].astype(F32) + got[here].astype(F32)
                copies.append(pltpu.make_async_copy(total.at[here], hbm.at[here], sum_sem.at[i, e, n]))
                copies[-1].start()
    for c in copies:
        c.wait()


def shards(mesh_shape, tokens, gate_probs, expert_ids, copies, weight_in, weight_out, cotangent):
    groups = mesh_shape["ex"]
    count, width = tokens.shape
    hidden = weight_in.shape[2]
    unit_rows = 12 * groups
    kind_rows = 6 * groups
    all_rows = UNITS * kind_rows
    pack = jnp.asarray(pack_matrix(groups), BF16)
    vmem, anywhere = pl.BlockSpec(memory_space=pltpu.VMEM), pl.BlockSpec(memory_space=pl.ANY)
    shape = jax.ShapeDtypeStruct
    dma = pltpu.SemaphoreType.DMA
    results = pl.pallas_call(
        functools.partial(layer_kernel, groups),
        out_shape=(
            shape((count, width), BF16), shape((count, width), BF16), shape((2, count), F32),
            shape(weight_in.shape, BF16), shape(weight_in.shape, BF16),
            shape(weight_out.shape, BF16), shape(weight_out.shape, BF16),
        ),
        in_specs=[pl.BlockSpec(memory_space=pltpu.HBM)] * 8,
        out_specs=(vmem, vmem, vmem, anywhere, anywhere, anywhere, anywhere),
        scratch_shapes=[
            pltpu.VMEM((2, count), jnp.int32), pltpu.SMEM(copies.shape, jnp.int32), pltpu.VMEM(pack.shape, BF16),
            pltpu.VMEM((count, width), BF16), pltpu.VMEM((count, width), BF16), pltpu.VMEM((2, count), F32),
            pltpu.VMEM((2,) + weight_in.shape, BF16),
            pltpu.VMEM((2,) + weight_out.shape, BF16),
            pltpu.VMEM((2, groups, FRAME, width), BF16),
            pltpu.VMEM((2, groups, FRAME, width), BF16),
            pltpu.VMEM((UNITS, unit_rows, width), BF16),
            pltpu.VMEM((UNITS, unit_rows, width), BF16),
            pltpu.VMEM((2, 15, kind_rows, width), BF16),
            pltpu.VMEM((unit_rows, width), BF16),
            pltpu.VMEM((2, groups, FRAME, width), BF16),
            pltpu.VMEM((2, groups, FRAME, width), BF16),
            pltpu.VMEM((all_rows, 2 * hidden), BF16),
            pltpu.VMEM((all_rows, 2 * hidden), BF16),
            pltpu.VMEM((all_rows, 2 * hidden), F32),
            pltpu.VMEM((2,) + weight_in.shape, BF16),
            pltpu.VMEM((2,) + weight_out.shape, BF16),
            dma((6,)), dma((2,)), dma((2,)), dma((2,)),
            dma((2, 2)), dma((2, 2, groups)),
            dma(()), dma((2, 2, 16)),
            dma(()), dma((2, 2, 16)),
            dma((2, 2)), dma((2, 2, groups)),
            dma((2,)), dma((2,)), dma((2,)),
        ],
        compiler_params=pltpu.CompilerParams(
            collective_id=0, has_side_effects=True, vmem_limit_bytes=46 * 2**20
        ),
        name="moe_layer",
    )(*(
        pltpu.with_memory_space_constraint(v, pltpu.HBM)
        for v in (expert_ids.T, copies, pack, tokens, cotangent, gate_probs.T, weight_in, weight_out)
    ))
    hbm = pl.BlockSpec(memory_space=pltpu.HBM)
    layer_out, grad_tokens, grad_gates, grad_in, grad_out = pl.pallas_call(
        finish_kernel,
        out_shape=(
            shape((count, width), BF16), shape((count, width), BF16), shape((2, count), F32),
            shape(weight_in.shape, F32), shape(weight_out.shape, F32),
        ),
        in_specs=[vmem] * 7,
        out_specs=(hbm,) * 5,
        scratch_shapes=[
            pltpu.VMEM(weight_in.shape, F32), pltpu.VMEM(weight_out.shape, F32), dma((3,)), dma((2, 2, 4)),
        ],
        compiler_params=pltpu.CompilerParams(vmem_limit_bytes=8 * 2**20),
        name="replica_sums",
    )(*(pltpu.with_memory_space_constraint(v, pltpu.VMEM) for v in results))
    return layer_out, grad_tokens, grad_gates.T, grad_in, grad_out


def solution(mesh):
    rows = P(("et", "ex", "dp"), None)
    w_in = P("ex", None, ("et", "dp"))
    w_out = P("ex", ("et", "dp"), None)
    return jax.shard_map(
        functools.partial(shards, dict(mesh.shape)),
        mesh=mesh,
        in_specs=(rows, rows, rows, P(), w_in, w_out, rows),
        out_specs=(rows, rows, rows, w_in, w_out),
        check_vma=False,
    )
```
